256 devices in a mesh: gx: 16 (over x, z_hi), gy: 4 (over z_lo, core), sa: 4 (over y).
Axes of the slice: x: 4, y: 4, z: 8 (z_hi: 4, z_lo: 2; z = z_hi * 2 + z_lo), core: 2. Of those that a mesh axis runs over, the one named last changes fastest.
Arguments:
- scalar_field: float32 [64, 1, 1024, 512], P('sa', None, 'gx', 'gy'), may hold values from -80 to 80, as said below
- start_basis: float32 [1024, 128], replicated, may hold values from -6 to 6
Outputs:
- core_tensor: float32 [64, 1, 128, 512], P(('sa', 'gx'), None, 'gy')
- leading_basis: float32 [1024, 128], P(('gx', 'gy', 'sa'))
The draws below stay inside these ranges and needn't reach their ends.
Inputs may be any that keep to these rules, and one draw needn't show every extreme that they name: `scalar_field`: every entry is finite.
All inputs are finite; a program needn't handle non-finite values.
Results may differ from the reference program's by a relative error of at most 0.0003.
Values sent between devices are 32-bit elements; how exact they have to be, the bound alone decides.
A program may use at most 64 MiB of HBM per device.

```python
import math
import jax
import jax.numpy as jnp
from jax import lax

NX = 1024
S = 64
R = 128
ITERS = 3
STEPS = 1
NY = 512


def draw_scalar_field(key, part):
    keys = jax.random.split(key, 5)
    shape = (S, STEPS, NX, NY)
    mode_count = R + R // 8
    decay = math.log(625.0) / (R - 1)
    floor_scale = math.sqrt(NX / 600.0)
    species_scale = jnp.exp(jax.random.uniform(keys[2], (S,), jnp.float32, 0.0, math.log(4.0)))
    noise = jnp.clip(jax.random.normal(keys[0], shape, jnp.float32), -4.0, 4.0)

    def add_mode(index, total):
        along_x = jnp.clip(jax.random.normal(jax.random.fold_in(keys[3], index), (NX,), jnp.float32), -3.0, 3.0)
        along_y = jnp.clip(jax.random.normal(jax.random.fold_in(keys[4], index), (S, STEPS, NY), jnp.float32), -3.0, 3.0)
        amplitude = jnp.exp(-0.5 * decay * index.astype(jnp.float32))
        return total + amplitude * along_y[:, :, None, :] * along_x[None, None, :, None]
    total = lax.fori_loop(0, mode_count, add_mode, floor_scale * noise)
    return jnp.clip(0.25 * total * species_scale[:, None, None, None], -80.0, 80.0)


def centred(stream_key, shape, scale, reach, dtype=jnp.bfloat16):
    result = jax.random.normal(stream_key, shape, jnp.float32) * scale
    return jnp.minimum(jnp.maximum(result, -reach), reach).astype(dtype)


def setup_inputs(seed: int = 0) -> dict:
    key_of = jax.random.split(jax.random.key(seed), 3)
    return {
        "scalar_field": draw_scalar_field(jax.random.fold_in(key_of[2], 71), 0),
        "start_basis": centred(key_of[1], (NX, R), 1.0, 6.0, jnp.float32),
    }


HIGHEST_PREC = lax.Precision.HIGHEST

def orthonormal(mapped):
    inner_gram = jnp.dot(mapped.T.astype(jnp.float32), mapped.astype(jnp.float32), precision=HIGHEST_PREC, preferred_element_type=jnp.float32)
    factor = jnp.linalg.cholesky(inner_gram)
    return jax.scipy.linalg.solve_triangular(factor, mapped.T, lower=True).T

def reference(scalar_field, start_basis):
    slabs = scalar_field.reshape(S * STEPS, NX, NY)

    def accumulate(carry, slab_now):
        return (carry + jnp.dot(slab_now.astype(jnp.float32), slab_now.T.astype(jnp.float32), precision=HIGHEST_PREC, preferred_element_type=jnp.float32), None)
    gram_matrix, _ = lax.scan(accumulate, jnp.zeros((NX, NX), jnp.float32), slabs)
    gram_matrix = gram_matrix / (NY * S * STEPS)
    cur_basis = start_basis
    for iteration in range(ITERS):
        mapped = jnp.dot(gram_matrix.astype(jnp.float32), cur_basis.astype(jnp.float32), precision=HIGHEST_PREC, preferred_element_type=jnp.float32)
        cur_basis = orthonormal(orthonormal(mapped))
    core_tensor = jnp.einsum('xk,stxy->stky', cur_basis.astype(jnp.float32), scalar_field.astype(jnp.float32), precision=HIGHEST_PREC, preferred_element_type=jnp.float32)
    return (core_tensor, cur_basis)
```

```python
import functools

import jax
import jax.numpy as jnp
from jax import lax
from jax.experimental import pallas as pl
from jax.experimental.pallas import tpu as pltpu
from jax.sharding import PartitionSpec as P

NX = 1024
S = 64
ITERS = 3


HIGHEST_PREC = lax.Precision.HIGHEST


def row_of(v, p):
    return jnp.broadcast_to(v[p:p + 1, :], v.shape)

def lane_of(v, c):
    return jnp.broadcast_to(v[:, c:c + 1], v.shape)

def inverse_factor(a_ref, rank):
    sub = lax.broadcasted_iota(jnp.int32, (8, rank), 0)
    lane = lax.broadcasted_iota(jnp.int32, (8, rank), 1)
    panels = rank // 8
    for k in range(panels):
        base = 8 * k
        more = k + 1 < panels
        panel = a_ref[base:base + 8, :]
        cols = [lane_of(panel, base + c) for c in range(8)]
        inside = (lane >= base) & (lane < base + 8)
        panel = jnp.where(inside, jnp.where(lane - base == sub, 1.0, 0.0), panel)
        if more:
            nxt = a_ref[base + 8:base + 16, :]
            ncols = [lane_of(nxt, base + c) for c in range(8)]
            nxt = jnp.where(inside, 0.0, nxt)
        diag = jnp.zeros((8, rank), jnp.float32)
        for p in range(8):
            d = row_of(cols[p], p)
            r = 1.0 / d
            diag = jnp.where(sub == p, d, diag)
            f = jnp.where(sub > p, cols[p] * r, 0.0)
            prow = row_of(panel, p)
            if more:
                g = ncols[p] * r
                nxt = nxt - g * prow
            if p < 7:
                for c in range(p + 1, 8):
                    crow = row_of(cols[c], p)
                    cols[c] = cols[c] - f * crow
                    if more:
                        ncols[c] = ncols[c] - g * crow
                panel = panel - f * prow
        root = lax.rsqrt(diag)
        scaled = panel * root
        a_ref[base:base + 8, :] = jnp.where(lane < base + 8, scaled, 0.0)
        if more:
            a_ref[base + 8:base + 16, :] = nxt
        if k + 2 < panels:
            low = base + 16
            upper = jnp.where(lane >= low, scaled, 0.0)
            upd = lax.dot_general(upper, scaled, (((0,), (0,)), ((), ())), precision=HIGHEST_PREC,
                                  preferred_element_type=jnp.float32)
            rest = a_ref[low:, :]
            lanes = lax.broadcasted_iota(jnp.int32, rest.shape, 1)
            rest = jnp.where((lanes >= base) & (lanes < base + 8), 0.0, rest)
            a_ref[low:, :] = rest - upd[low:, :]

def iterate_body(iters, g_ref, q0_ref, q_ref, y_ref, a_ref):
    rows, rank = q0_ref.shape
    tile = 256
    q_ref[...] = q0_ref[...]

    @pl.loop(0, iters)
    def _(it):
        @pl.loop(0, rows // tile)
        def _(t):
            at = pl.ds(pl.multiple_of(t * tile, tile), tile)
            y_ref[at, :] = jnp.dot(g_ref[at, :], q_ref[...], precision=HIGHEST_PREC, preferred_element_type=jnp.float32)
        q_ref[...] = y_ref[...]

        @pl.loop(0, 2)
        def _(twice):
            y = q_ref[...]
            a_ref[...] = lax.dot_general(y, y, (((0,), (0,)), ((), ())), precision=HIGHEST_PREC,
                                         preferred_element_type=jnp.float32)
            inverse_factor(a_ref, rank)
            q_ref[...] = lax.dot_general(q_ref[...], a_ref[...], (((1,), (1,)), ((), ())), precision=HIGHEST_PREC,
                                         preferred_element_type=jnp.float32)

def iterate(gram, start, iters):
    rows, rank = start.shape
    return pl.pallas_call(
        functools.partial(iterate_body, iters),
        out_shape=jax.ShapeDtypeStruct((rows, rank), jnp.float32),
        in_specs=[pl.BlockSpec(memory_space=pltpu.VMEM)] * 2,
        out_specs=pl.BlockSpec(memory_space=pltpu.VMEM),
        scratch_shapes=[pltpu.VMEM((rows, rank), jnp.float32), pltpu.VMEM((rank, rank), jnp.float32)],
        compiler_params=pltpu.CompilerParams(vmem_limit_bytes=40 * 1024 * 1024),
        name="iterate",
    )(gram, start)


def on_device(scalar_field, start_basis):
    fibres = lax.all_to_all(scalar_field, "gx", split_axis=0, concat_axis=2, tiled=True)
    total_cols = fibres.shape[3] * lax.axis_size("gy") * S * fibres.shape[1]
    devices = lax.axis_size(("gx", "gy", "sa"))
    rows_dev = NX // devices
    my_index = lax.axis_index(("gx", "gy", "sa"))
    partial_value = jnp.einsum(
        "stxy,stzy->xz", fibres, fibres, precision=HIGHEST_PREC, preferred_element_type=jnp.float32
    )
    gram_matrix = lax.psum(partial_value, ("gx", "gy", "sa")) / total_cols
    cur_basis = iterate(gram_matrix, start_basis, ITERS)
    own_rows = lax.dynamic_slice_in_dim(cur_basis, my_index * rows_dev, rows_dev, 0)
    projected = jnp.einsum(
        "xk,stxy->stky",
        cur_basis,
        fibres,
        precision=HIGHEST_PREC,
        preferred_element_type=jnp.float32,
    )
    core_tensor = lax.all_to_all(projected, "gy", split_axis=2, concat_axis=3, tiled=True)
    return (core_tensor, own_rows)


def solution(mesh):
    placed = (P("sa", None, "gx", "gy"), P())
    return jax.shard_map(
        on_device,
        mesh=mesh,
        in_specs=placed,
        out_specs=(P(("sa", "gx"), None, "gy", None), P(("gx", "gy", "sa"), None)),
        check_vma=False,
    )
```

```python
import functools

import jax
import jax.numpy as jnp
from jax import lax
from jax.experimental import pallas as pl
from jax.experimental.pallas import tpu as pltpu
from jax.sharding import PartitionSpec as P

NX = 1024
S = 64
ITERS = 3


HIGHEST_PREC = lax.Precision.HIGHEST


def row_of(v, p):
    return jnp.broadcast_to(v[p:p + 1, :], v.shape)

def lane_of(v, c):
    return jnp.broadcast_to(v[:, c:c + 1], v.shape)

def inverse_factor(a_ref, rank):
    sub = lax.broadcasted_iota(jnp.int32, (8, rank), 0)
    lane = lax.broadcasted_iota(jnp.int32, (8, rank), 1)
    panels = rank // 8
    for k in range(panels):
        base = 8 * k
        more = k + 1 < panels
        panel = a_ref[base:base + 8, :]
        cols = [lane_of(panel, base + c) for c in range(8)]
        inside = (lane >= base) & (lane < base + 8)
        panel = jnp.where(inside, jnp.where(lane - base == sub, 1.0, 0.0), panel)
        if more:
            nxt = a_ref[base + 8:base + 16, :]
            ncols = [lane_of(nxt, base + c) for c in range(8)]
            nxt = jnp.where(inside, 0.0, nxt)
        diag = jnp.zeros((8, rank), jnp.float32)
        for p in range(8):
            d = row_of(cols[p], p)
            r = 1.0 / d
            diag = jnp.where(sub == p, d, diag)
            f = jnp.where(sub > p, cols[p] * r, 0.0)
            prow = row_of(panel, p)
            if more:
                g = ncols[p] * r
                nxt = nxt - g * prow
            if p < 7:
                for c in range(p + 1, 8):
                    crow = row_of(cols[c], p)
                    cols[c] = cols[c] - f * crow
                    if more:
                        ncols[c] = ncols[c] - g * crow
                panel = panel - f * prow
        root = lax.rsqrt(diag)
        scaled = panel * root
        a_ref[base:base + 8, :] = jnp.where(lane < base + 8, scaled, 0.0)
        if more:
            a_ref[base + 8:base + 16, :] = nxt
        if k + 2 < panels:
            low = base + 16
            upper = jnp.where(lane >= low, scaled, 0.0)
            upd = lax.dot_general(upper, scaled, (((0,), (0,)), ((), ())), precision=HIGHEST_PREC,
                                  preferred_element_type=jnp.float32)
            rest = a_ref[low:, :]
            lanes = lax.broadcasted_iota(jnp.int32, rest.shape, 1)
            rest = jnp.where((lanes >= base) & (lanes < base + 8), 0.0, rest)
            a_ref[low:, :] = rest - upd[low:, :]

def iterate_body(iters, g_ref, q0_ref, q_ref, y_ref, a_ref):
    rows, rank = q0_ref.shape
    tile = 256
    q_ref[...] = q0_ref[...]

    @pl.loop(0, iters)
    def _(it):
        @pl.loop(0, rows // tile)
        def _(t):
            at = pl.ds(pl.multiple_of(t * tile, tile), tile)
            y_ref[at, :] = jnp.dot(g_ref[at, :], q_ref[...], precision=HIGHEST_PREC, preferred_element_type=jnp.float32)
        q_ref[...] = y_ref[...]

        @pl.loop(0, 2)
        def _(twice):
            y = q_ref[...]
            a_ref[...] = lax.dot_general(y, y, (((0,), (0,)), ((), ())), precision=HIGHEST_PREC,
                                         preferred_element_type=jnp.float32)
            inverse_factor(a_ref, rank)
            q_ref[...] = lax.dot_general(q_ref[...], a_ref[...], (((1,), (1,)), ((), ())), precision=HIGHEST_PREC,
                                         preferred_element_type=jnp.float32)

def iterate(gram, start, iters):
    rows, rank = start.shape
    return pl.pallas_call(
        functools.partial(iterate_body, iters),
        out_shape=jax.ShapeDtypeStruct((rows, rank), jnp.float32),
        in_specs=[pl.BlockSpec(memory_space=pltpu.VMEM)] * 2,
        out_specs=pl.BlockSpec(memory_space=pltpu.VMEM),
        scratch_shapes=[pltpu.VMEM((rows, rank), jnp.float32), pltpu.VMEM((rank, rank), jnp.float32)],
        compiler_params=pltpu.CompilerParams(vmem_limit_bytes=40 * 1024 * 1024),
        name="iterate",
    )(gram, start)


MESH = pl.DeviceIdType.MESH

def place():
    gx, gy, sa = lax.axis_index("gx"), lax.axis_index("gy"), lax.axis_index("sa")
    return gx // 4, sa, (gx % 4) * 2 + gy // 2, gy % 2

def device_at(x, y, z, core):
    return {"gx": x * 4 + z // 2, "gy": (z % 2) * 2 + core, "sa": y}

def gram_body(scale, f_ref, out_ref, cat, part, r0, r1, r2, r3, zout, zin, zall,
              cat_sems, rs_send, rs_recv, zr_send, zr_recv, za_send, za_recv,
              ag_send, ag_recv, core_send, core_recv):
    x, y, z, core = place()
    rbufs = (r0, r1, r2, r3)
    mate = device_at(x, y, z, 1 - core)
    pair = lambda i: i + 1 - 2 * (i % 2)
    dims = (
        (((x + 1) // 2) % 2, device_at(pair(x), y, z, core)),
        (((y + 1) // 2) % 2, device_at(x, pair(y), z, core)),
        (x // 2, device_at(3 - x, y, z, core)),
        (y // 2, device_at(x, 3 - y, z, core)),
    )
    zpeers = [device_at(x, y, (z + o) % 8, core) for o in range(1, 8)]

    barrier = pltpu.get_barrier_semaphore()
    peers = [mate] + [d[1] for d in dims] + zpeers
    for peer in peers:
        pl.semaphore_signal(barrier, inc=1, device_id=peer, device_id_type=MESH)
    pl.semaphore_wait(barrier, len(peers))

    def remote(src, dst, ss, rs, dev):
        return pltpu.make_async_remote_copy(src_ref=src, dst_ref=dst, send_sem=ss, recv_sem=rs,
                                            device_id=dev, device_id_type=MESH)
    swap = remote(f_ref, cat.at[:, pl.ds(128, 128)], cat_sems.at[0], cat_sems.at[1], mate)
    swap.start()
    cat[:, 0:128] = f_ref[...]
    swap.wait()

    sent = []
    offs = []
    for q in range(4):
        o = [0]
        for s in range(4):
            bit = dims[(q + s) % 4][0]
            o.append(o[-1] + bit * (64 >> s))
        offs.append(o)

    def halve(q, s):
        half = 64 >> s
        bit, dev = dims[(q + s) % 4]
        row = pl.multiple_of(offs[q][s] + (1 - bit) * half, 8)
        return remote(part.at[q, pl.ds(row, half), :], rbufs[s].at[q],
                      rs_send.at[s, q], rs_recv.at[s, q], dev)

    top = core * 512
    for q in range(4):
        lhs = cat[pl.ds(pl.multiple_of(top + q * 128, 128), 128), :]
        part[q] = lax.dot_general(lhs, cat[...], (((1,), (1,)), ((), ())), precision=HIGHEST_PREC,
                                  preferred_element_type=jnp.float32)
        c = halve(q, 0)
        c.start()
        sent.append(c)
    for s in range(4):
        half = 64 >> s
        for q in range(4):
            halve(q, s).wait_recv()
            keep = pl.ds(pl.multiple_of(offs[q][s + 1], 8), half)
            part[q, keep, :] = part[q, keep, :] + rbufs[s][q]
            if s < 3:
                c = halve(q, s + 1)
                c.start()
                sent.append(c)
    for q in range(4):
        rows = pl.ds(pl.multiple_of(offs[q][4], 8), 8)
        for t in range(8):
            zout[t, q] = part[q, rows, 128 * t:128 * t + 128]
    def zscatter(o):
        return remote(zout.at[(z + o) % 8], zin.at[o - 1], zr_send.at[o - 1], zr_recv.at[o - 1], zpeers[o - 1])
    def zgather(o):
        return remote(zall.at[0], zall.at[o], za_send.at[o - 1], za_recv.at[o - 1], zpeers[o - 1])
    for o in range(1, 8):
        c = zscatter(o)
        c.start()
        sent.append(c)
    total = zout[z]
    for o in range(1, 8):
        zscatter(o).wait_recv()
        total = total + zin[o - 1]
    zall[0] = total * scale
    for o in range(1, 8):
        c = zgather(o)
        c.start()
        sent.append(c)

    def at_row(q, row, size):
        return pl.ds(pl.multiple_of(top + q * 128 + row, 8), size)

    for o in range(8):
        if o:
            zgather(o).wait_recv()
        lanes = pl.ds(pl.multiple_of(((z + 8 - o) % 8) * 128, 128), 128)
        for q in range(4):
            out_ref[at_row(q, offs[q][4], 8), lanes] = zall[o, q]

    def grow(q, s):
        ref = out_ref.at[at_row(q, offs[q][s + 1], 64 >> s), :]
        return remote(ref, ref, ag_send.at[s, q], ag_recv.at[s, q], dims[(q + s) % 4][1])

    def hand(q, s):
        if s == 4:
            rows = at_row(q, offs[q][4], 8)
        else:
            half = 64 >> s
            rows = at_row(q, offs[q][s] + (1 - dims[(q + s) % 4][0]) * half, half)
        ref = out_ref.at[rows, :]
        return remote(ref, ref, core_send.at[s, q], core_recv.at[s, q], mate)

    def take(q, s):
        if s == 4:
            row, size = offs[q][4], 8
        else:
            size = 64 >> s
            row = offs[q][s] + (1 - dims[(q + s) % 4][0]) * size
        ref = out_ref.at[pl.ds(pl.multiple_of(512 - top + q * 128 + row, 8), size), :]
        return remote(ref, ref, core_send.at[s, q], core_recv.at[s, q], mate)

    for s in (3, 2, 1, 0):
        for q in range(4):
            if s < 3:
                grown = offs[q][s + 1] + (1 - dims[(q + s + 1) % 4][0]) * (64 >> (s + 1))
                ref = out_ref.at[at_row(q, grown, 64 >> (s + 1)), :]
                remote(ref, ref, ag_send.at[s + 1, q], ag_recv.at[s + 1, q], mate).wait_recv()
            c = grow(q, s)
            c.start()
            sent.append(c)
            c = hand(q, s + 1)
            c.start()
            sent.append(c)
    for q in range(4):
        grown = offs[q][0] + (1 - dims[q % 4][0]) * 64
        ref = out_ref.at[at_row(q, grown, 64), :]
        remote(ref, ref, ag_send.at[0, q], ag_recv.at[0, q], mate).wait_recv()
        c = hand(q, 0)
        c.start()
        sent.append(c)
    for s in (4, 3, 2, 1, 0):
        for q in range(4):
            take(q, s).wait_recv()
    for c in sent:
        c.wait_send()

def summed_gram(fibre, scale):
    nx, width = fibre.shape
    dma = lambda *shape: pltpu.SemaphoreType.DMA(shape)
    vm = lambda *shape: pltpu.VMEM(shape, jnp.float32)
    return pl.pallas_call(
        functools.partial(gram_body, scale),
        out_shape=jax.ShapeDtypeStruct((nx, nx), jnp.float32),
        in_specs=[pl.BlockSpec(memory_space=pltpu.VMEM)],
        out_specs=pl.BlockSpec(memory_space=pltpu.VMEM),
        scratch_shapes=[
            vm(nx, 2 * width), vm(4, 128, nx),
            vm(4, 64, nx), vm(4, 32, nx), vm(4, 16, nx), vm(4, 8, nx),
            vm(8, 4, 8, 128), vm(7, 4, 8, 128), vm(8, 4, 8, 128),
            dma(2), dma(4, 4), dma(4, 4), dma(7), dma(7), dma(7), dma(7),
            dma(4, 4), dma(4, 4), dma(5, 4), dma(5, 4),
        ],
        compiler_params=pltpu.CompilerParams(collective_id=0, has_side_effects=True,
                                             vmem_limit_bytes=40 * 1024 * 1024),
        name="summed_gram",
    )(fibre)


def on_device(scalar_field, start_basis):
    fibres = lax.all_to_all(scalar_field, "gx", split_axis=0, concat_axis=2, tiled=True)
    total_cols = fibres.shape[3] * lax.axis_size("gy") * S * fibres.shape[1]
    devices = lax.axis_size(("gx", "gy", "sa"))
    rows_dev = NX // devices
    my_index = lax.axis_index(("gx", "gy", "sa"))
    gram_matrix = summed_gram(fibres.reshape(NX, fibres.shape[3]), 1.0 / total_cols)
    cur_basis = iterate(gram_matrix, start_basis, ITERS)
    own_rows = lax.dynamic_slice_in_dim(cur_basis, my_index * rows_dev, rows_dev, 0)
    projected = jnp.einsum(
        "xk,stxy->stky",
        cur_basis,
        fibres,
        precision=HIGHEST_PREC,
        preferred_element_type=jnp.float32,
    )
    core_tensor = lax.all_to_all(projected, "gy", split_axis=2, concat_axis=3, tiled=True)
    return (core_tensor, own_rows)


def solution(mesh):
    placed = (P("sa", None, "gx", "gy"), P())
    return jax.shard_map(
        on_device,
        mesh=mesh,
        in_specs=placed,
        out_specs=(P(("sa", "gx"), None, "gy", None), P(("gx", "gy", "sa"), None)),
        check_vma=False,
    )
```

```python
import functools

import jax
import jax.numpy as jnp
from jax import lax
from jax.experimental import pallas as pl
from jax.experimental.pallas import tpu as pltpu
from jax.sharding import PartitionSpec as P

NX = 1024
S = 64
ITERS = 3

HI = lax.Precision.HIGHEST
MESH = pl.DeviceIdType.MESH

def place():
    gx, gy, sa = lax.axis_index("gx"), lax.axis_index("gy"), lax.axis_index("sa")
    return gx // 4, sa, (gx % 4) * 2 + gy // 2, gy % 2

def device_at(x, y, z, core):
    return {"gx": x * 4 + z // 2, "gy": (z % 2) * 2 + core, "sa": y}


def row_of(v, p):
    return jnp.broadcast_to(v[p:p + 1, :], v.shape)

def lane_of(v, c):
    return jnp.broadcast_to(v[:, c:c + 1], v.shape)

def inverse_factor(a_ref, rank):
    sub = lax.broadcasted_iota(jnp.int32, (8, rank), 0)
    lane = lax.broadcasted_iota(jnp.int32, (8, rank), 1)
    panels = rank // 8
    for k in range(panels):
        base = 8 * k
        more = k + 1 < panels
        panel = a_ref[base:base + 8, :]
        cols = [lane_of(panel, base + c) for c in range(8)]
        inside = (lane >= base) & (lane < base + 8)
        panel = jnp.where(inside, jnp.where(lane - base == sub, 1.0, 0.0), panel)
        if more:
            nxt = a_ref[base + 8:base + 16, :]
            ncols = [lane_of(nxt, base + c) for c in range(8)]
            nxt = jnp.where(inside, 0.0, nxt)
        diag = jnp.zeros((8, rank), jnp.float32)
        for p in range(8):
            d = row_of(cols[p], p)
            r = 1.0 / d
            diag = jnp.where(sub == p, d, diag)
            f = jnp.where(sub > p, cols[p] * r, 0.0)
            prow = row_of(panel, p)
            if more:
                g = ncols[p] * r
                nxt = nxt - g * prow
            if p < 7:
                for c in range(p + 1, 8):
                    crow = row_of(cols[c], p)
                    cols[c] = cols[c] - f * crow
                    if more:
                        ncols[c] = ncols[c] - g * crow
                panel = panel - f * prow
        root = lax.rsqrt(diag)
        scaled = panel * root
        a_ref[base:base + 8, :] = jnp.where(lane < base + 8, scaled, 0.0)
        if more:
            a_ref[base + 8:base + 16, :] = nxt
        if k + 2 < panels:
            low = base + 16
            upper = jnp.where(lane >= low, scaled, 0.0)
            upd = lax.dot_general(upper, scaled, (((0,), (0,)), ((), ())), precision=HI,
                                  preferred_element_type=jnp.float32)
            rest = a_ref[low:, :]
            lanes = lax.broadcasted_iota(jnp.int32, rest.shape, 1)
            rest = jnp.where((lanes >= base) & (lanes < base + 8), 0.0, rest)
            a_ref[low:, :] = rest - upd[low:, :]


def split(v):
    high = v.astype(jnp.bfloat16)
    return high, (v - high.astype(jnp.float32)).astype(jnp.bfloat16)


def dot3(a, b, contract):
    one = lambda u, v: lax.dot_general(u, v, (contract, ((), ())), preferred_element_type=jnp.float32)
    return one(a[0], b[0]) + (one(a[0], b[1]) + one(a[1], b[0]))


def whole_body(scale, iters, field_ref, q0_ref, core_ref, rows_ref, own, other, high, low, part, r0, r1, r2, r3,
               zout, zin, zall, out_ref, q_ref, y_ref, a_ref, proj,
               fs_send, fs_recv, fw_send, fw_recv, rs_send, rs_recv, zr_send, zr_recv, za_send, za_recv,
               ag_send, ag_recv, core_send, core_recv, last_sems):
    x, y, z, core = place()
    rbufs = (r0, r1, r2, r3)
    mate = device_at(x, y, z, 1 - core)
    pair = lambda i: i + 1 - 2 * (i % 2)
    dims = (
        (((x + 1) // 2) % 2, device_at(pair(x), y, z, core)),
        (((y + 1) // 2) % 2, device_at(x, pair(y), z, core)),
        (x // 2, device_at(3 - x, y, z, core)),
        (y // 2, device_at(x, 3 - y, z, core)),
    )
    zpeers = [device_at(x, y, (z + o) % 8, core) for o in range(1, 8)]

    barrier = pltpu.get_barrier_semaphore()
    gx, gy, sa = lax.axis_index("gx"), lax.axis_index("gy"), lax.axis_index("sa")
    xpeers = [{"gx": (gx + o) % 16, "gy": gy, "sa": sa} for o in range(1, 16)]
    peers = [mate, dims[1][1], dims[3][1]] + zpeers[0::2] + xpeers
    for peer in peers:
        pl.semaphore_signal(barrier, inc=1, device_id=peer, device_id_type=MESH)
    pl.semaphore_wait(barrier, len(peers))

    def remote(src, dst, ss, rs, dev):
        return pltpu.make_async_remote_copy(src_ref=src, dst_ref=dst, send_sem=ss, recv_sem=rs,
                                            device_id=dev, device_id_type=MESH)
    sent = []

    def spread(o):
        return remote(field_ref.at[(gx + o) % 16], own.at[gx], fs_send.at[o - 1], fs_recv.at[o - 1], xpeers[o - 1])

    def forward(o):
        block = (gx + 16 - o) % 16
        src = own.at[block] if o else field_ref.at[block]
        return remote(src, other.at[block], fw_send.at[o], fw_recv.at[o], mate)

    order = (8, 4, 12, 6, 10, 7, 9, 5, 11, 2, 14, 3, 13, 1, 15)
    for o in order:
        c = spread(o)
        c.start()
        sent.append(c)
    c = forward(0)
    c.start()
    sent.append(c)

    def store(block, values, lanes):
        rows = pl.ds(pl.multiple_of(block * 64, 64), 64)
        high[rows, lanes], low[rows, lanes] = split(values)

    mine, its = slice(0, 128), slice(128, 256)
    store(gx, field_ref[gx], mine)
    for o in reversed(order):
        block = (gx + 16 - o) % 16
        spread(o).wait_recv()
        c = forward(o)
        c.start()
        sent.append(c)
        store(block, own[block], mine)
    for o in (0,) + order[::-1]:
        block = (gx + 16 - o) % 16
        remote(field_ref.at[0], other.at[block], fw_send.at[o], fw_recv.at[o], mate).wait_recv()
        store(block, other[block], its)

    offs = []
    for q in range(4):
        o = [0]
        for s in range(4):
            bit = dims[(q + s) % 4][0]
            o.append(o[-1] + bit * (64 >> s))
        offs.append(o)

    def halve(q, s):
        half = 64 >> s
        bit, dev = dims[(q + s) % 4]
        row = pl.multiple_of(offs[q][s] + (1 - bit) * half, 8)
        return remote(part.at[q, pl.ds(row, half), :], rbufs[s].at[q],
                      rs_send.at[s, q], rs_recv.at[s, q], dev)

    top = core * 512
    for q in range(4):
        rows = pl.ds(pl.multiple_of(top + q * 128, 128), 128)
        part[q] = dot3((high[rows, :], low[rows, :]), (high[...], low[...]), ((1,), (1,)))
        c = halve(q, 0)
        c.start()
        sent.append(c)
    for s in range(4):
        half = 64 >> s
        for q in range(4):
            halve(q, s).wait_recv()
            keep = pl.ds(pl.multiple_of(offs[q][s + 1], 8), half)
            part[q, keep, :] = part[q, keep, :] + rbufs[s][q]
            if s < 3:
                c = halve(q, s + 1)
                c.start()
                sent.append(c)
    for q in range(4):
        rows = pl.ds(pl.multiple_of(offs[q][4], 8), 8)
        for t in range(8):
            zout[t, q] = part[q, rows, 128 * t:128 * t + 128]
    def zscatter(o):
        return remote(zout.at[(z + o) % 8], zin.at[o - 1], zr_send.at[o - 1], zr_recv.at[o - 1], zpeers[o - 1])
    def zgather(o):
        return remote(zall.at[0], zall.at[o], za_send.at[o - 1], za_recv.at[o - 1], zpeers[o - 1])
    for o in range(1, 8):
        c = zscatter(o)
        c.start()
        sent.append(c)
    total = zout[z]
    for o in range(1, 8):
        zscatter(o).wait_recv()
        total = total + zin[o - 1]
    zall[0] = total * scale
    for o in range(1, 8):
        c = zgather(o)
        c.start()
        sent.append(c)

    def at_row(q, row, size):
        return pl.ds(pl.multiple_of(top + q * 128 + row, 8), size)

    for o in range(8):
        if o:
            zgather(o).wait_recv()
        lanes = pl.ds(pl.multiple_of(((z + 8 - o) % 8) * 128, 128), 128)
        for q in range(4):
            out_ref[at_row(q, offs[q][4], 8), lanes] = zall[o, q]

    def grow(q, s):
        ref = out_ref.at[at_row(q, offs[q][s + 1], 64 >> s), :]
        return remote(ref, ref, ag_send.at[s, q], ag_recv.at[s, q], dims[(q + s) % 4][1])

    def hand(q, s):
        if s == 4:
            rows = at_row(q, offs[q][4], 8)
        else:
            half = 64 >> s
            rows = at_row(q, offs[q][s] + (1 - dims[(q + s) % 4][0]) * half, half)
        ref = out_ref.at[rows, :]
        return remote(ref, ref, core_send.at[s, q], core_recv.at[s, q], mate)

    def take(q, s):
        if s == 4:
            row, size = offs[q][4], 8
        else:
            size = 64 >> s
            row = offs[q][s] + (1 - dims[(q + s) % 4][0]) * size
        ref = out_ref.at[pl.ds(pl.multiple_of(512 - top + q * 128 + row, 8), size), :]
        return remote(ref, ref, core_send.at[s, q], core_recv.at[s, q], mate)

    for s in (3, 2, 1, 0):
        for q in range(4):
            if s < 3:
                grown = offs[q][s + 1] + (1 - dims[(q + s + 1) % 4][0]) * (64 >> (s + 1))
                ref = out_ref.at[at_row(q, grown, 64 >> (s + 1)), :]
                remote(ref, ref, ag_send.at[s + 1, q], ag_recv.at[s + 1, q], mate).wait_recv()
            c = grow(q, s)
            c.start()
            sent.append(c)
            c = hand(q, s + 1)
            c.start()
            sent.append(c)
    for q in range(4):
        grown = offs[q][0] + (1 - dims[q % 4][0]) * 64
        ref = out_ref.at[at_row(q, grown, 64), :]
        remote(ref, ref, ag_send.at[0, q], ag_recv.at[0, q], mate).wait_recv()
        c = hand(q, 0)
        c.start()
        sent.append(c)
    for s in (4, 3, 2, 1, 0):
        for q in range(4):
            take(q, s).wait_recv()

    rows, rank = q0_ref.shape
    tile = 256
    q_ref[...] = q0_ref[...]

    @pl.loop(0, iters)
    def _(it):
        @pl.loop(0, rows // tile)
        def _(t):
            at = pl.ds(pl.multiple_of(t * tile, tile), tile)
            y_ref[at, :] = jnp.dot(out_ref[at, :], q_ref[...], precision=HI, preferred_element_type=jnp.float32)

        q_ref[...] = y_ref[...]

        @pl.loop(0, 2)
        def _(twice):
            mapped = q_ref[...]
            a_ref[...] = lax.dot_general(mapped, mapped, (((0,), (0,)), ((), ())), precision=HI,
                                         preferred_element_type=jnp.float32)
            inverse_factor(a_ref, rank)
            q_ref[...] = lax.dot_general(q_ref[...], a_ref[...], (((1,), (1,)), ((), ())), precision=HI,
                                         preferred_element_type=jnp.float32)

    basis = split(q_ref[...])
    made = dot3(basis, (high[...], low[...]), ((0,), (0,)))
    share = rank // 4
    width = 128
    for t in range(4):
        proj[t, :, pl.ds(pl.multiple_of(core * width, width), width)] = made[t * share:(t + 1) * share, 0:width]
        proj[t, :, pl.ds(pl.multiple_of((1 - core) * width, width), width)] = made[t * share:(t + 1) * share, width:]
    zl = z % 2
    span = pl.ds(pl.multiple_of(zl * 2 * width, 2 * width), 2 * width)
    c = remote(proj.at[(1 - zl) * 2 + core], core_ref.at[:, span], last_sems.at[0], last_sems.at[1],
               device_at(x, y, z + 1 - 2 * zl, core))
    c.start()
    core_ref[:, span] = proj[gy]
    index = (gx * 4 + gy) * 4 + sa
    block = q_ref[pl.ds(pl.multiple_of((index // 2) * 8, 8), 8), :]
    flag = jnp.broadcast_to(index % 2, (4, rank))
    rows_ref[...] = jnp.where(flag == 0, block[0:4, :], block[4:8, :])
    c.wait_recv()
    sent.append(c)
    for c in sent:
        c.wait_send()


def whole(field, start, scale, iters):
    species, nx, width = field.shape[0], start.shape[0], field.shape[2]
    rank = start.shape[1]
    dma = lambda *shape: pltpu.SemaphoreType.DMA(shape)
    vm = lambda *shape: pltpu.VMEM(shape, jnp.float32)
    half = lambda *shape: pltpu.VMEM(shape, jnp.bfloat16)
    return pl.pallas_call(
        functools.partial(whole_body, scale, iters),
        out_shape=(jax.ShapeDtypeStruct((rank // 4, 4 * width), jnp.float32),
                   jax.ShapeDtypeStruct((nx // 256, rank), jnp.float32)),
        in_specs=[pl.BlockSpec(memory_space=pltpu.VMEM)] * 2,
        out_specs=(pl.BlockSpec(memory_space=pltpu.VMEM),) * 2,
        scratch_shapes=[
            vm(16, 64, width), vm(16, 64, width), half(nx, 2 * width), half(nx, 2 * width), vm(4, 128, nx),
            vm(4, 64, nx), vm(4, 32, nx), vm(4, 16, nx), vm(4, 8, nx),
            vm(8, 4, 8, 128), vm(7, 4, 8, 128), vm(8, 4, 8, 128), vm(nx, nx),
            vm(nx, rank), vm(nx, rank), vm(rank, rank), vm(4, rank // 4, 2 * width),
            dma(15), dma(15), dma(16), dma(16), dma(4, 4), dma(4, 4), dma(7), dma(7), dma(7), dma(7),
            dma(4, 4), dma(4, 4), dma(5, 4), dma(5, 4), dma(2),
        ],
        compiler_params=pltpu.CompilerParams(collective_id=0, has_side_effects=True,
                                             vmem_limit_bytes=48 * 1024 * 1024),
        name="whole",
    )(field, start)


def on_device(scalar_field, start_basis):
    species, steps, rows, width = scalar_field.shape
    total_cols = width * lax.axis_size("gy") * S * steps
    core_tensor, own_rows = whole(scalar_field.reshape(species, rows, width), start_basis, 1.0 / total_cols, ITERS)
    return (core_tensor.reshape(1, steps, *core_tensor.shape), own_rows)


def solution(mesh):
    placed = (P("sa", None, "gx", "gy"), P())
    return jax.shard_map(
        on_device,
        mesh=mesh,
        in_specs=placed,
        out_specs=(P(("sa", "gx"), None, "gy", None), P(("gx", "gy", "sa"), None)),
        check_vma=False,
    )
```

```python
import functools

import jax
import jax.numpy as jnp
from jax import lax
from jax.experimental import pallas as pl
from jax.experimental.pallas import tpu as pltpu
from jax.sharding import PartitionSpec as P

NX = 1024
S = 64
ITERS = 3

HI = lax.Precision.HIGHEST
MESH = pl.DeviceIdType.MESH

def place():
    gx, gy, sa = lax.axis_index("gx"), lax.axis_index("gy"), lax.axis_index("sa")
    return gx // 4, sa, (gx % 4) * 2 + gy // 2, gy % 2

def device_at(x, y, z, core):
    return {"gx": x * 4 + z // 2, "gy": (z % 2) * 2 + core, "sa": y}


def row_of(v, p):
    return jnp.broadcast_to(v[p:p + 1, :], v.shape)

def lane_of(v, c):
    return jnp.broadcast_to(v[:, c:c + 1], v.shape)

def inverse_factor(a_ref, rank):
    sub = lax.broadcasted_iota(jnp.int32, (8, rank), 0)
    lane = lax.broadcasted_iota(jnp.int32, (8, rank), 1)
    panels = rank // 8
    for k in range(panels):
        base = 8 * k
        more = k + 1 < panels
        panel = a_ref[base:base + 8, :]
        cols = [lane_of(panel, base + c) for c in range(8)]
        inside = (lane >= base) & (lane < base + 8)
        panel = jnp.where(inside, jnp.where(lane - base == sub, 1.0, 0.0), panel)
        if more:
            nxt = a_ref[base + 8:base + 16, :]
            ncols = [lane_of(nxt, base + c) for c in range(8)]
            nxt = jnp.where(inside, 0.0, nxt)
        diag = jnp.zeros((8, rank), jnp.float32)
        for p in range(8):
            d = row_of(cols[p], p)
            r = 1.0 / d
            diag = jnp.where(sub == p, d, diag)
            f = jnp.where(sub > p, cols[p] * r, 0.0)
            prow = row_of(panel, p)
            if more:
                g = ncols[p] * r
                nxt = nxt - g * prow
            if p < 7:
                for c in range(p + 1, 8):
                    crow = row_of(cols[c], p)
                    cols[c] = cols[c] - f * crow
                    if more:
                        ncols[c] = ncols[c] - g * crow
                panel = panel - f * prow
        root = lax.rsqrt(diag)
        scaled = panel * root
        a_ref[base:base + 8, :] = jnp.where(lane < base + 8, scaled, 0.0)
        if more:
            a_ref[base + 8:base + 16, :] = nxt
        if k + 2 < panels:
            low = base + 16
            upper = jnp.where(lane >= low, scaled, 0.0)
            upd = lax.dot_general(upper, scaled, (((0,), (0,)), ((), ())), precision=HI,
                                  preferred_element_type=jnp.float32)
            rest = a_ref[low:, :]
            lanes = lax.broadcasted_iota(jnp.int32, rest.shape, 1)
            rest = jnp.where((lanes >= base) & (lanes < base + 8), 0.0, rest)
            a_ref[low:, :] = rest - upd[low:, :]


def split(v):
    high = v.astype(jnp.bfloat16)
    return high, (v - high.astype(jnp.float32)).astype(jnp.bfloat16)


def thirds(v):
    big, rest = v.astype(jnp.bfloat16), v
    rest = rest - big.astype(jnp.float32)
    mid = rest.astype(jnp.bfloat16)
    return big, mid, (rest - mid.astype(jnp.float32)).astype(jnp.bfloat16)


def dot3(a, b, contract):
    one = lambda u, v: lax.dot_general(u, v, (contract, ((), ())), preferred_element_type=jnp.float32)
    return one(a[0], b[0]) + (one(a[0], b[1]) + one(a[1], b[0]))


def whole_body(scale, iters, field_ref, q0_ref, core_ref, rows_ref, own, other, high, low, part, r0, r1, r2, r3,
               zout, zin, zall, gsym, gram, parts_q, q_ref, a_ref, proj,
               fs_send, fs_recv, fw_send, fw_recv, rs_send, rs_recv, zr_send, zr_recv, za_send, za_recv,
               ag_send, ag_recv, core_send, core_recv, last_sems):
    x, y, z, core = place()
    rbufs = (r0, r1, r2, r3)
    mate = device_at(x, y, z, 1 - core)
    pair = lambda i: i + 1 - 2 * (i % 2)
    dims = (
        (((x + 1) // 2) % 2, device_at(pair(x), y, z, core)),
        (((y + 1) // 2) % 2, device_at(x, pair(y), z, core)),
        (x // 2, device_at(3 - x, y, z, core)),
        (y // 2, device_at(x, 3 - y, z, core)),
    )
    zpeers = [device_at(x, y, (z + o) % 8, core) for o in range(1, 8)]

    barrier = pltpu.get_barrier_semaphore()
    gx, gy, sa = lax.axis_index("gx"), lax.axis_index("gy"), lax.axis_index("sa")
    xpeers = [{"gx": (gx + o) % 16, "gy": gy, "sa": sa} for o in range(1, 16)]
    peers = [mate, dims[1][1], dims[3][1]] + zpeers[0::2] + xpeers
    for peer in peers:
        pl.semaphore_signal(barrier, inc=1, device_id=peer, device_id_type=MESH)
    pl.semaphore_wait(barrier, len(peers))

    def remote(src, dst, ss, rs, dev):
        return pltpu.make_async_remote_copy(src_ref=src, dst_ref=dst, send_sem=ss, recv_sem=rs,
                                            device_id=dev, device_id_type=MESH)
    sent = []

    def spread(o):
        return remote(field_ref.at[(gx + o) % 16], own.at[gx], fs_send.at[o - 1], fs_recv.at[o - 1], xpeers[o - 1])

    def forward(o):
        block = (gx + 16 - o) % 16
        src = own.at[block] if o else field_ref.at[block]
        return remote(src, other.at[block], fw_send.at[o], fw_recv.at[o], mate)

    order = (8, 4, 12, 6, 10, 7, 9, 5, 11, 2, 14, 3, 13, 1, 15)
    for o in order:
        c = spread(o)
        c.start()
        sent.append(c)
    c = forward(0)
    c.start()
    sent.append(c)

    def store(block, values, lanes):
        halves = split(values)
        for first in (0, 1024):
            rows = pl.ds(pl.multiple_of(block * 64 + first, 64), 64)
            high[rows, lanes], low[rows, lanes] = halves

    mine, its = slice(0, 128), slice(128, 256)
    store(gx, field_ref[gx], mine)
    for o in reversed(order):
        block = (gx + 16 - o) % 16
        spread(o).wait_recv()
        c = forward(o)
        c.start()
        sent.append(c)
        store(block, own[block], mine)
    for o in (0,) + order[::-1]:
        block = (gx + 16 - o) % 16
        remote(field_ref.at[0], other.at[block], fw_send.at[o], fw_recv.at[o], mate).wait_recv()
        store(block, other[block], its)

    offs = []
    for q in range(4):
        o = [0]
        for s in range(4):
            bit = dims[(q + s) % 4][0]
            o.append(o[-1] + bit * (64 >> s))
        offs.append(o)

    def halve(q, s):
        half = 64 >> s
        bit, dev = dims[(q + s) % 4]
        row = pl.multiple_of(offs[q][s] + (1 - bit) * half, 8)
        return remote(part.at[q, pl.ds(row, half), :], rbufs[s].at[q],
                      rs_send.at[s, q], rs_recv.at[s, q], dev)

    top = core * 512
    for q in range(4):
        rows = pl.ds(pl.multiple_of(top + q * 128, 128), 128)
        window = pl.ds(pl.multiple_of(top + q * 128, 128), 640)
        part[q] = dot3((high[rows, :], low[rows, :]), (high[window, :], low[window, :]), ((1,), (1,)))
        c = halve(q, 0)
        c.start()
        sent.append(c)
    for s in range(4):
        half = 64 >> s
        for q in range(4):
            halve(q, s).wait_recv()
            keep = pl.ds(pl.multiple_of(offs[q][s + 1], 8), half)
            part[q, keep, :] = part[q, keep, :] + rbufs[s][q]
            if s < 3:
                c = halve(q, s + 1)
                c.start()
                sent.append(c)
    for n in range(24):
        q, lanes = n // 5, slice(128 * (n % 5), 128 * (n % 5) + 128)
        if n < 20:
            zout[n % 8, n // 8] = part[q, pl.ds(pl.multiple_of(offs[q][4], 8), 8), lanes]
        else:
            zout[n % 8, n // 8] = jnp.zeros((8, 128), jnp.float32)

    def zscatter(o):
        return remote(zout.at[(z + o) % 8], zin.at[o - 1], zr_send.at[o - 1], zr_recv.at[o - 1], zpeers[o - 1])
    def zgather(o):
        return remote(zall.at[0], zall.at[o], za_send.at[o - 1], za_recv.at[o - 1], zpeers[o - 1])
    for o in range(1, 8):
        c = zscatter(o)
        c.start()
        sent.append(c)
    total = zout[z]
    for o in range(1, 8):
        zscatter(o).wait_recv()
        total = total + zin[o - 1]
    zall[0] = total * scale
    for o in range(1, 8):
        c = zgather(o)
        c.start()
        sent.append(c)

    def at_row(q, row, size):
        return pl.ds(pl.multiple_of(top + q * 128 + row, 8), size)

    for o in range(1, 8):
        zgather(o).wait_recv()
    for n in range(20):
        q, lanes = n // 5, slice(128 * (n % 5), 128 * (n % 5) + 128)
        gsym[at_row(q, offs[q][4], 8), lanes] = zall[(z + 8 - n % 8) % 8, n // 8]

    def grow(q, s):
        ref = gsym.at[at_row(q, offs[q][s + 1], 64 >> s), :]
        return remote(ref, ref, ag_send.at[s, q], ag_recv.at[s, q], dims[(q + s) % 4][1])

    def hand(q, s):
        if s == 4:
            rows = at_row(q, offs[q][4], 8)
        else:
            half = 64 >> s
            rows = at_row(q, offs[q][s] + (1 - dims[(q + s) % 4][0]) * half, half)
        ref = gsym.at[rows, :]
        return remote(ref, ref, core_send.at[s, q], core_recv.at[s, q], mate)

    def take(q, s):
        if s == 4:
            row, size = offs[q][4], 8
        else:
            size = 64 >> s
            row = offs[q][s] + (1 - dims[(q + s) % 4][0]) * size
        ref = gsym.at[pl.ds(pl.multiple_of(512 - top + q * 128 + row, 8), size), :]
        return remote(ref, ref, core_send.at[s, q], core_recv.at[s, q], mate)

    for s in (3, 2, 1, 0):
        for q in range(4):
            if s < 3:
                grown = offs[q][s + 1] + (1 - dims[(q + s + 1) % 4][0]) * (64 >> (s + 1))
                ref = gsym.at[at_row(q, grown, 64 >> (s + 1)), :]
                remote(ref, ref, ag_send.at[s + 1, q], ag_recv.at[s + 1, q], mate).wait_recv()
            c = grow(q, s)
            c.start()
            sent.append(c)
            c = hand(q, s + 1)
            c.start()
            sent.append(c)
    for q in range(4):
        grown = offs[q][0] + (1 - dims[q % 4][0]) * 64
        ref = gsym.at[at_row(q, grown, 64), :]
        remote(ref, ref, ag_send.at[0, q], ag_recv.at[0, q], mate).wait_recv()
        c = hand(q, 0)
        c.start()
        sent.append(c)
    for s in (4, 3, 2, 1, 0):
        for q in range(4):
            take(q, s).wait_recv()

    rows, rank = q0_ref.shape
    tile = 256
    q_ref[...] = q0_ref[...]
    for i in range(8):
        for b in range(5):
            j = (i + b) % 8
            block = gsym[128 * i:128 * i + 128, 128 * b:128 * b + 128]
            spots = [(i, j, block)]
            if 0 < b < 4:
                spots.append((j, i, block.T))
            for row, col, value in spots:
                for n, piece in enumerate(thirds(value)):
                    gram[n, 128 * row:128 * row + 128, 128 * col:128 * col + 128] = piece

    @pl.loop(0, iters)
    def _(it):
        for n, piece in enumerate(thirds(q_ref[...])):
            parts_q[:, 128 * n:128 * n + 128] = piece

        @pl.loop(0, rows // tile)
        def _(t):
            at = pl.ds(pl.multiple_of(t * tile, tile), tile)
            one = lambda u, v: jnp.dot(u, v, preferred_element_type=jnp.float32)
            big, mid, small = gram[0, at, :], gram[1, at, :], gram[2, at, :]
            both = parts_q[:, 0:256]
            wide = one(big, both) + one(mid, both)
            tiny = one(big, parts_q[:, 256:384]) + one(small, parts_q[:, 0:128])
            q_ref[at, :] = wide[:, 0:128] + (wide[:, 128:256] + tiny)

        @pl.loop(0, 2)
        def _(twice):
            mapped = q_ref[...]
            a_ref[...] = lax.dot_general(mapped, mapped, (((0,), (0,)), ((), ())), precision=HI,
                                         preferred_element_type=jnp.float32)
            inverse_factor(a_ref, rank)
            q_ref[...] = lax.dot_general(q_ref[...], a_ref[...], (((1,), (1,)), ((), ())), precision=HI,
                                         preferred_element_type=jnp.float32)

    basis = split(q_ref[...])
    made = dot3(basis, (high[0:rows, :], low[0:rows, :]), ((0,), (0,)))
    share = rank // 4
    width = 128
    for t in range(4):
        proj[t, :, pl.ds(pl.multiple_of(core * width, width), width)] = made[t * share:(t + 1) * share, 0:width]
        proj[t, :, pl.ds(pl.multiple_of((1 - core) * width, width), width)] = made[t * share:(t + 1) * share, width:]
    zl = z % 2
    span = pl.ds(pl.multiple_of(zl * 2 * width, 2 * width), 2 * width)
    c = remote(proj.at[(1 - zl) * 2 + core], core_ref.at[:, span], last_sems.at[0], last_sems.at[1],
               device_at(x, y, z + 1 - 2 * zl, core))
    c.start()
    core_ref[:, span] = proj[gy]
    index = (gx * 4 + gy) * 4 + sa
    block = q_ref[pl.ds(pl.multiple_of((index // 2) * 8, 8), 8), :]
    flag = jnp.broadcast_to(index % 2, (4, rank))
    rows_ref[...] = jnp.where(flag == 0, block[0:4, :], block[4:8, :])
    c.wait_recv()
    sent.append(c)
    for c in sent:
        c.wait_send()


def whole(field, start, scale, iters):
    species, nx, width = field.shape[0], start.shape[0], field.shape[2]
    rank = start.shape[1]
    dma = lambda *shape: pltpu.SemaphoreType.DMA(shape)
    vm = lambda *shape: pltpu.VMEM(shape, jnp.float32)
    half = lambda *shape: pltpu.VMEM(shape, jnp.bfloat16)
    return pl.pallas_call(
        functools.partial(whole_body, scale, iters),
        out_shape=(jax.ShapeDtypeStruct((rank // 4, 4 * width), jnp.float32),
                   jax.ShapeDtypeStruct((nx // 256, rank), jnp.float32)),
        in_specs=[pl.BlockSpec(memory_space=pltpu.VMEM)] * 2,
        out_specs=(pl.BlockSpec(memory_space=pltpu.VMEM),) * 2,
        scratch_shapes=[
            vm(16, 64, width), vm(16, 64, width), half(2 * nx, 2 * width), half(2 * nx, 2 * width),
            vm(4, 128, 640), vm(4, 64, 640), vm(4, 32, 640), vm(4, 16, 640), vm(4, 8, 640),
            vm(8, 3, 8, 128), vm(7, 3, 8, 128), vm(8, 3, 8, 128), vm(nx, 640),
            half(3, nx, nx), half(nx, 3 * rank), vm(nx, rank), vm(rank, rank), vm(4, rank // 4, 2 * width),
            dma(15), dma(15), dma(16), dma(16), dma(4, 4), dma(4, 4), dma(7), dma(7), dma(7), dma(7),
            dma(4, 4), dma(4, 4), dma(5, 4), dma(5, 4), dma(2),
        ],
        compiler_params=pltpu.CompilerParams(collective_id=0, has_side_effects=True,
                                             vmem_limit_bytes=48 * 1024 * 1024),
        name="whole",
    )(field, start)


def on_device(scalar_field, start_basis):
    species, steps, rows, width = scalar_field.shape
    total_cols = width * lax.axis_size("gy") * S * steps
    core_tensor, own_rows = whole(scalar_field.reshape(species, rows, width), start_basis, 1.0 / total_cols, ITERS)
    return (core_tensor.reshape(1, steps, *core_tensor.shape), own_rows)


def solution(mesh):
    placed = (P("sa", None, "gx", "gy"), P())
    return jax.shard_map(
        on_device,
        mesh=mesh,
        in_specs=placed,
        out_specs=(P(("sa", "gx"), None, "gy", None), P(("gx", "gy", "sa"), None)),
        check_vma=False,
    )
```

```python
import functools

import jax
import jax.numpy as jnp
from jax import lax
from jax.experimental import pallas as pl
from jax.experimental.pallas import tpu as pltpu
from jax.sharding import PartitionSpec as P

NX = 1024
S = 64
ITERS = 3

TOP = float(jnp.finfo(jnp.float32).max)
MESH = pl.DeviceIdType.MESH

def place():
    gx, gy, sa = lax.axis_index("gx"), lax.axis_index("gy"), lax.axis_index("sa")
    return gx // 4, sa, (gx % 4) * 2 + gy // 2, gy % 2

def device_at(x, y, z, core):
    return {"gx": x * 4 + z // 2, "gy": (z % 2) * 2 + core, "sa": y}


def row_of(v, p):
    return jnp.broadcast_to(v[p:p + 1, :], v.shape)

def lane_of(v, c):
    return jnp.minimum(jnp.broadcast_to(v[:, c:c + 1], v.shape), TOP)

def inverse_factor(a_ref, rank):
    sub = lax.broadcasted_iota(jnp.int32, (8, rank), 0)
    lane = lax.broadcasted_iota(jnp.int32, (8, rank), 1)
    panels = rank // 8
    for k in range(panels):
        base = 8 * k
        more = k + 1 < panels
        panel = a_ref[base:base + 8, :]
        cols = [lane_of(panel, base + c) for c in range(8)]
        inside = (lane >= base) & (lane < base + 8)
        panel = jnp.where(inside, jnp.where(lane - base == sub, 1.0, 0.0), panel)
        if more:
            nxt = a_ref[base + 8:base + 16, :]
            ncols = [lane_of(nxt, base + c) for c in range(8)]
            nxt = jnp.where(inside, 0.0, nxt)
        diag = jnp.zeros((8, rank), jnp.float32)
        for p in range(8):
            d = row_of(cols[p], p)
            r = 1.0 / d
            diag = jnp.where(sub == p, d, diag)
            f = jnp.where(sub > p, cols[p] * r, 0.0)
            prow = row_of(panel, p)
            if more:
                g = ncols[p] * r
                nxt = nxt - g * prow
            if p < 7:
                for c in range(p + 1, 8):
                    crow = row_of(cols[c], p)
                    cols[c] = cols[c] - f * crow
                    if more:
                        ncols[c] = ncols[c] - g * crow
                panel = panel - f * prow
        root = lax.rsqrt(diag)
        scaled = panel * root
        a_ref[base:base + 8, :] = jnp.where(lane < base + 8, scaled, 0.0)
        if more:
            a_ref[base + 8:base + 16, :] = nxt
        if k + 2 < panels:
            low = base + 16
            upper = jnp.where(lane >= low, scaled, 0.0)
            left, right = thirds(upper), thirds(scaled)
            pick = lambda v, order: jnp.concatenate([v[n].astype(jnp.float32) for n in order]).astype(jnp.bfloat16)
            upd = lax.dot_general(pick(left, (0, 0, 1, 1, 0, 2)), pick(right, (0, 1, 0, 1, 2, 0)),
                                  (((0,), (0,)), ((), ())), preferred_element_type=jnp.float32)
            rest = a_ref[low:, :]
            lanes = lax.broadcasted_iota(jnp.int32, rest.shape, 1)
            rest = jnp.where((lanes >= base) & (lanes < base + 8), 0.0, rest)
            a_ref[low:, :] = rest - upd[low:, :]


def split(v):
    high = v.astype(jnp.bfloat16)
    return high, (v - high.astype(jnp.float32)).astype(jnp.bfloat16)


def thirds(v):
    big, rest = v.astype(jnp.bfloat16), v
    rest = rest - big.astype(jnp.float32)
    mid = rest.astype(jnp.bfloat16)
    return big, mid, (rest - mid.astype(jnp.float32)).astype(jnp.bfloat16)


def dot3(a, b, contract):
    one = lambda u, v: lax.dot_general(u, v, (contract, ((), ())), preferred_element_type=jnp.float32)
    return one(a[0], b[0]) + (one(a[0], b[1]) + one(a[1], b[0]))


def whole_body(scale, iters, field_ref, q0_ref, core_ref, rows_ref, own, other, high, low, part, r0, r1, r2, r3,
               zout, zin, zall, gsym, gram, parts_q, q_ref, a_ref, proj,
               fs_send, fs_recv, fw_send, fw_recv, rs_send, rs_recv, zr_send, zr_recv, za_send, za_recv,
               ag_send, ag_recv, core_send, core_recv, last_sems):
    x, y, z, core = place()
    rbufs = (r0, r1, r2, r3)
    mate = device_at(x, y, z, 1 - core)
    pair = lambda i: i + 1 - 2 * (i % 2)
    dims = (
        (((x + 1) // 2) % 2, device_at(pair(x), y, z, core)),
        (((y + 1) // 2) % 2, device_at(x, pair(y), z, core)),
        (x // 2, device_at(3 - x, y, z, core)),
        (y // 2, device_at(x, 3 - y, z, core)),
    )
    zpeers = [device_at(x, y, (z + o) % 8, core) for o in range(1, 8)]

    barrier = pltpu.get_barrier_semaphore()
    gx, gy, sa = lax.axis_index("gx"), lax.axis_index("gy"), lax.axis_index("sa")
    xpeers = [{"gx": (gx + o) % 16, "gy": gy, "sa": sa} for o in range(1, 16)]
    peers = [mate, dims[1][1], dims[3][1]] + zpeers[0::2] + xpeers
    for peer in peers:
        pl.semaphore_signal(barrier, inc=1, device_id=peer, device_id_type=MESH)
    pl.semaphore_wait(barrier, len(peers))

    def remote(src, dst, ss, rs, dev):
        return pltpu.make_async_remote_copy(src_ref=src, dst_ref=dst, send_sem=ss, recv_sem=rs,
                                            device_id=dev, device_id_type=MESH)
    sent = []

    def spread(o):
        return remote(field_ref.at[(gx + o) % 16], own.at[gx], fs_send.at[o - 1], fs_recv.at[o - 1], xpeers[o - 1])

    def forward(o):
        block = (gx + 16 - o) % 16
        src = own.at[block] if o else field_ref.at[block]
        return remote(src, other.at[block], fw_send.at[o], fw_recv.at[o], mate)

    order = (8, 4, 12, 6, 10, 7, 9, 5, 11, 2, 14, 3, 13, 1, 15)
    for o in order:
        c = spread(o)
        c.start()
        sent.append(c)
    c = forward(0)
    c.start()
    sent.append(c)

    def store(block, values, lanes):
        halves = split(values)
        for first in (0, 1024):
            rows = pl.ds(pl.multiple_of(block * 64 + first, 64), 64)
            high[rows, lanes], low[rows, lanes] = halves

    mine, its = slice(0, 128), slice(128, 256)
    store(gx, field_ref[gx], mine)
    for o in reversed(order):
        block = (gx + 16 - o) % 16
        spread(o).wait_recv()
        c = forward(o)
        c.start()
        sent.append(c)
        store(block, own[block], mine)
    for o in (0,) + order[::-1]:
        block = (gx + 16 - o) % 16
        remote(field_ref.at[0], other.at[block], fw_send.at[o], fw_recv.at[o], mate).wait_recv()
        store(block, other[block], its)

    offs = []
    for q in range(4):
        o = [0]
        for s in range(4):
            bit = dims[(q + s) % 4][0]
            o.append(o[-1] + bit * (64 >> s))
        offs.append(o)

    def halve(q, s):
        half = 64 >> s
        bit, dev = dims[(q + s) % 4]
        row = pl.multiple_of(offs[q][s] + (1 - bit) * half, 8)
        return remote(part.at[q, pl.ds(row, half), :], rbufs[s].at[q],
                      rs_send.at[s, q], rs_recv.at[s, q], dev)

    top = core * 512
    for q in range(4):
        rows = pl.ds(pl.multiple_of(top + q * 128, 128), 128)
        window = pl.ds(pl.multiple_of(top + q * 128, 128), 640)
        part[q] = dot3((high[rows, :], low[rows, :]), (high[window, :], low[window, :]), ((1,), (1,)))
        c = halve(q, 0)
        c.start()
        sent.append(c)
    for s in range(4):
        half = 64 >> s
        for q in range(4):
            halve(q, s).wait_recv()
            keep = pl.ds(pl.multiple_of(offs[q][s + 1], 8), half)
            part[q, keep, :] = part[q, keep, :] + rbufs[s][q]
            if s < 3:
                c = halve(q, s + 1)
                c.start()
                sent.append(c)
    for n in range(24):
        q, lanes = n // 5, slice(128 * (n % 5), 128 * (n % 5) + 128)
        if n < 20:
            zout[n % 8, n // 8] = part[q, pl.ds(pl.multiple_of(offs[q][4], 8), 8), lanes]
        else:
            zout[n % 8, n // 8] = jnp.zeros((8, 128), jnp.float32)

    def zscatter(o):
        return remote(zout.at[(z + o) % 8], zin.at[o - 1], zr_send.at[o - 1], zr_recv.at[o - 1], zpeers[o - 1])
    def zgather(o):
        return remote(zall.at[0], zall.at[o], za_send.at[o - 1], za_recv.at[o - 1], zpeers[o - 1])
    for o in range(1, 8):
        c = zscatter(o)
        c.start()
        sent.append(c)
    total = zout[z]
    for o in range(1, 8):
        zscatter(o).wait_recv()
        total = total + zin[o - 1]
    zall[0] = total * scale
    for o in range(1, 8):
        c = zgather(o)
        c.start()
        sent.append(c)

    def at_row(q, row, size):
        return pl.ds(pl.multiple_of(top + q * 128 + row, 8), size)

    for o in range(1, 8):
        zgather(o).wait_recv()
    for n in range(20):
        q, lanes = n // 5, slice(128 * (n % 5), 128 * (n % 5) + 128)
        gsym[at_row(q, offs[q][4], 8), lanes] = zall[(z + 8 - n % 8) % 8, n // 8]

    def grow(q, s):
        ref = gsym.at[at_row(q, offs[q][s + 1], 64 >> s), :]
        return remote(ref, ref, ag_send.at[s, q], ag_recv.at[s, q], dims[(q + s) % 4][1])

    def hand(q, s):
        if s == 4:
            rows = at_row(q, offs[q][4], 8)
        else:
            half = 64 >> s
            rows = at_row(q, offs[q][s] + (1 - dims[(q + s) % 4][0]) * half, half)
        ref = gsym.at[rows, :]
        return remote(ref, ref, core_send.at[s, q], core_recv.at[s, q], mate)

    def take(q, s):
        if s == 4:
            row, size = offs[q][4], 8
        else:
            size = 64 >> s
            row = offs[q][s] + (1 - dims[(q + s) % 4][0]) * size
        ref = gsym.at[pl.ds(pl.multiple_of(512 - top + q * 128 + row, 8), size), :]
        return remote(ref, ref, core_send.at[s, q], core_recv.at[s, q], mate)

    for s in (3, 2, 1, 0):
        for q in range(4):
            if s < 3:
                grown = offs[q][s + 1] + (1 - dims[(q + s + 1) % 4][0]) * (64 >> (s + 1))
                ref = gsym.at[at_row(q, grown, 64 >> (s + 1)), :]
                remote(ref, ref, ag_send.at[s + 1, q], ag_recv.at[s + 1, q], mate).wait_recv()
            c = grow(q, s)
            c.start()
            sent.append(c)
            c = hand(q, s + 1)
            c.start()
            sent.append(c)
    for q in range(4):
        grown = offs[q][0] + (1 - dims[q % 4][0]) * 64
        ref = gsym.at[at_row(q, grown, 64), :]
        remote(ref, ref, ag_send.at[0, q], ag_recv.at[0, q], mate).wait_recv()
        c = hand(q, 0)
        c.start()
        sent.append(c)
    for s in (4, 3, 2, 1, 0):
        for q in range(4):
            take(q, s).wait_recv()

    rows, rank = q0_ref.shape
    tile = 256
    one = lambda u, v: jnp.dot(u, v, preferred_element_type=jnp.float32)

    def keep(at, values):
        for n, piece in enumerate(thirds(values)):
            parts_q[at, 128 * n:128 * n + 128] = piece

    keep(slice(0, rows), q0_ref[...])
    for i in range(8):
        for b in range(5):
            j = (i + b) % 8
            block = gsym[128 * i:128 * i + 128, 128 * b:128 * b + 128]
            spots = [(i, j, block)]
            if 0 < b < 4:
                spots.append((j, i, block.T))
            for row, col, value in spots:
                for n, piece in enumerate(thirds(value)):
                    gram[n, 128 * row:128 * row + 128, 128 * col:128 * col + 128] = piece

    @pl.loop(0, iters)
    def _(it):
        @pl.loop(0, rows // tile)
        def _(t):
            at = pl.ds(pl.multiple_of(t * tile, tile), tile)
            big, mid, small = gram[0, at, :], gram[1, at, :], gram[2, at, :]
            both = parts_q[:, 0:256]
            wide = one(big, both) + one(mid, both)
            tiny = one(big, parts_q[:, 256:384]) + one(small, parts_q[:, 0:128])
            q_ref[at, :] = wide[:, 0:128] + (wide[:, 128:256] + tiny)

        keep(slice(0, rows), q_ref[...])

        @pl.loop(0, 2)
        def _(twice):
            inner = lambda u, v: lax.dot_general(u, v, (((0,), (0,)), ((), ())), preferred_element_type=jnp.float32)
            both = parts_q[:, 0:256]
            four = inner(both, both)
            cross = inner(parts_q[:, 0:128], parts_q[:, 256:384]) + four[0:128, 128:256]
            a_ref[...] = four[0:128, 0:128] + ((cross + cross.T) + four[128:256, 128:256])
            inverse_factor(a_ref, rank)
            f_big, f_mid, f_small = thirds(a_ref[...].T)
            main = jnp.concatenate([jnp.concatenate([f_big, f_big]), jnp.concatenate([f_mid, f_mid])], axis=1)
            wide = one(parts_q[:, 0:256], main)
            tiny = one(parts_q[:, 0:128], f_small) + one(parts_q[:, 256:384], f_big)
            q_ref[...] = wide[:, 0:128] + (wide[:, 128:256] + tiny)
            keep(slice(0, rows), q_ref[...])

    basis = (parts_q[:, 0:128], parts_q[:, 128:256])
    made = dot3(basis, (high[0:rows, :], low[0:rows, :]), ((0,), (0,)))
    share = rank // 4
    width = 128
    for t in range(4):
        proj[t, :, pl.ds(pl.multiple_of(core * width, width), width)] = made[t * share:(t + 1) * share, 0:width]
        proj[t, :, pl.ds(pl.multiple_of((1 - core) * width, width), width)] = made[t * share:(t + 1) * share, width:]
    zl = z % 2
    span = pl.ds(pl.multiple_of(zl * 2 * width, 2 * width), 2 * width)
    c = remote(proj.at[(1 - zl) * 2 + core], core_ref.at[:, span], last_sems.at[0], last_sems.at[1],
               device_at(x, y, z + 1 - 2 * zl, core))
    c.start()
    core_ref[:, span] = proj[gy]
    index = (gx * 4 + gy) * 4 + sa
    block = q_ref[pl.ds(pl.multiple_of((index // 2) * 8, 8), 8), :]
    flag = jnp.broadcast_to(index % 2, (4, rank))
    rows_ref[...] = jnp.where(flag == 0, block[0:4, :], block[4:8, :])
    c.wait_recv()
    sent.append(c)
    for c in sent:
        c.wait_send()


def whole(field, start, scale, iters):
    species, nx, width = field.shape[0], start.shape[0], field.shape[2]
    rank = start.shape[1]
    dma = lambda *shape: pltpu.SemaphoreType.DMA(shape)
    vm = lambda *shape: pltpu.VMEM(shape, jnp.float32)
    half = lambda *shape: pltpu.VMEM(shape, jnp.bfloat16)
    return pl.pallas_call(
        functools.partial(whole_body, scale, iters),
        out_shape=(jax.ShapeDtypeStruct((rank // 4, 4 * width), jnp.float32),
                   jax.ShapeDtypeStruct((nx // 256, rank), jnp.float32)),
        in_specs=[pl.BlockSpec(memory_space=pltpu.VMEM)] * 2,
        out_specs=(pl.BlockSpec(memory_space=pltpu.VMEM),) * 2,
        scratch_shapes=[
            vm(16, 64, width), vm(16, 64, width), half(2 * nx, 2 * width), half(2 * nx, 2 * width),
            vm(4, 128, 640), vm(4, 64, 640), vm(4, 32, 640), vm(4, 16, 640), vm(4, 8, 640),
            vm(8, 3, 8, 128), vm(7, 3, 8, 128), vm(8, 3, 8, 128), vm(nx, 640),
            half(3, nx, nx), half(nx, 3 * rank), vm(nx, rank), vm(rank, rank), vm(4, rank // 4, 2 * width),
            dma(15), dma(15), dma(16), dma(16), dma(4, 4), dma(4, 4), dma(7), dma(7), dma(7), dma(7),
            dma(4, 4), dma(4, 4), dma(5, 4), dma(5, 4), dma(2),
        ],
        compiler_params=pltpu.CompilerParams(collective_id=0, has_side_effects=True,
                                             vmem_limit_bytes=48 * 1024 * 1024),
        name="whole",
    )(field, start)


def on_device(scalar_field, start_basis):
    species, steps, rows, width = scalar_field.shape
    total_cols = width * lax.axis_size("gy") * S * steps
    core_tensor, own_rows = whole(scalar_field.reshape(species, rows, width), start_basis, 1.0 / total_cols, ITERS)
    return (core_tensor.reshape(1, steps, *core_tensor.shape), own_rows)


def solution(mesh):
    placed = (P("sa", None, "gx", "gy"), P())
    return jax.shard_map(
        on_device,
        mesh=mesh,
        in_specs=placed,
        out_specs=(P(("sa", "gx"), None, "gy", None), P(("gx", "gy", "sa"), None)),
        check_vma=False,
    )
```

```python
import functools

import jax
import jax.numpy as jnp
from jax import lax
from jax.experimental import pallas as pl
from jax.experimental.pallas import tpu as pltpu
from jax.sharding import PartitionSpec as P

NX = 1024
S = 64
ITERS = 3

TOP = float(jnp.finfo(jnp.float32).max)
MESH = pl.DeviceIdType.MESH

def place():
    gx, gy, sa = lax.axis_index("gx"), lax.axis_index("gy"), lax.axis_index("sa")
    return gx // 4, sa, (gx % 4) * 2 + gy // 2, gy % 2

def device_at(x, y, z, core):
    return {"gx": x * 4 + z // 2, "gy": (z % 2) * 2 + core, "sa": y}


def row_of(v, p):
    return jnp.broadcast_to(v[p:p + 1, :], v.shape)

def lane_of(v, c):
    return jnp.minimum(jnp.broadcast_to(v[:, c:c + 1], v.shape), TOP)

def inverse_factor(a_ref, rank):
    sub = lax.broadcasted_iota(jnp.int32, (8, rank), 0)
    lane = lax.broadcasted_iota(jnp.int32, (8, rank), 1)
    panels = rank // 8
    for k in range(panels):
        base = 8 * k
        more = k + 1 < panels
        panel = a_ref[base:base + 8, :]
        cols = [lane_of(panel, base + c) for c in range(8)]
        inside = (lane >= base) & (lane < base + 8)
        panel = jnp.where(inside, jnp.where(lane - base == sub, 1.0, 0.0), panel)
        if more:
            nxt = a_ref[base + 8:base + 16, :]
            ncols = [lane_of(nxt, base + c) for c in range(8)]
            nxt = jnp.where(inside, 0.0, nxt)
        diag = jnp.zeros((8, rank), jnp.float32)
        for p in range(8):
            d = row_of(cols[p], p)
            r = 1.0 / d
            diag = jnp.where(sub == p, d, diag)
            f = jnp.where(sub > p, cols[p] * r, 0.0)
            prow = row_of(panel, p)
            if more:
                g = ncols[p] * r
                nxt = nxt - g * prow
            if p < 7:
                for c in range(p + 1, 8):
                    crow = row_of(cols[c], p)
                    cols[c] = cols[c] - f * crow
                    if more:
                        ncols[c] = ncols[c] - g * crow
                panel = panel - f * prow
        root = lax.rsqrt(diag)
        scaled = panel * root
        a_ref[base:base + 8, :] = jnp.where(lane < base + 8, scaled, 0.0)
        if more:
            a_ref[base + 8:base + 16, :] = nxt
        if k + 2 < panels:
            low = base + 16
            upper = jnp.where(lane >= low, scaled, 0.0)
            left, right = thirds(upper), thirds(scaled)
            pick = lambda v, order: jnp.concatenate([v[n].astype(jnp.float32) for n in order]).astype(jnp.bfloat16)
            upd = lax.dot_general(pick(left, (0, 0, 1, 1, 0, 2)), pick(right, (0, 1, 0, 1, 2, 0)),
                                  (((0,), (0,)), ((), ())), preferred_element_type=jnp.float32)
            rest = a_ref[low:, :]
            lanes = lax.broadcasted_iota(jnp.int32, rest.shape, 1)
            rest = jnp.where((lanes >= base) & (lanes < base + 8), 0.0, rest)
            a_ref[low:, :] = rest - upd[low:, :]


def split(v):
    high = v.astype(jnp.bfloat16)
    return high, (v - high.astype(jnp.float32)).astype(jnp.bfloat16)


def thirds(v):
    big, rest = v.astype(jnp.bfloat16), v
    rest = rest - big.astype(jnp.float32)
    mid = rest.astype(jnp.bfloat16)
    return big, mid, (rest - mid.astype(jnp.float32)).astype(jnp.bfloat16)


def dot3(a, b, contract):
    one = lambda u, v: lax.dot_general(u, v, (contract, ((), ())), preferred_element_type=jnp.float32)
    return one(a[0], b[0]) + (one(a[0], b[1]) + one(a[1], b[0]))


def whole_body(scale, iters, field_ref, q0_ref, core_ref, rows_ref, own, other, high, low, part, r0, r1, r2, r3,
               zout, zin, zall, gsym, gram, parts_q, q_ref, a_ref, proj,
               fs_send, fs_recv, fw_send, fw_recv, rs_send, rs_recv, zr_send, zr_recv, za_send, za_recv,
               ag_send, ag_recv, core_send, core_recv, last_sems, local_sems):
    x, y, z, core = place()
    rbufs = (r0, r1, r2, r3)
    mate = device_at(x, y, z, 1 - core)
    pair = lambda i: i + 1 - 2 * (i % 2)
    dims = (
        (((x + 1) // 2) % 2, device_at(pair(x), y, z, core)),
        (((y + 1) // 2) % 2, device_at(x, pair(y), z, core)),
        (x // 2, device_at(3 - x, y, z, core)),
        (y // 2, device_at(x, 3 - y, z, core)),
    )
    zpeers = [device_at(x, y, (z + o) % 8, core) for o in range(1, 8)]

    load_own = pltpu.make_async_copy(field_ref.at[lax.axis_index("gx")], own.at[lax.axis_index("gx")],
                                     local_sems.at[0])
    load_own.start()
    load_start = pltpu.make_async_copy(q0_ref, q_ref, local_sems.at[1])
    load_start.start()
    barrier = pltpu.get_barrier_semaphore()
    gx, gy, sa = lax.axis_index("gx"), lax.axis_index("gy"), lax.axis_index("sa")
    xpeers = [{"gx": (gx + o) % 16, "gy": gy, "sa": sa} for o in range(1, 16)]
    peers = [mate, dims[1][1], dims[3][1]] + zpeers[0::2] + xpeers
    for peer in peers:
        pl.semaphore_signal(barrier, inc=1, device_id=peer, device_id_type=MESH)
    pl.semaphore_wait(barrier, len(peers))

    def remote(src, dst, ss, rs, dev):
        return pltpu.make_async_remote_copy(src_ref=src, dst_ref=dst, send_sem=ss, recv_sem=rs,
                                            device_id=dev, device_id_type=MESH)
    sent = []

    def spread(o):
        return remote(field_ref.at[(gx + o) % 16], own.at[gx], fs_send.at[o - 1], fs_recv.at[o - 1], xpeers[o - 1])

    def forward(o):
        block = (gx + 16 - o) % 16
        return remote(own.at[block], other.at[block], fw_send.at[o], fw_recv.at[o], mate)

    order = (8, 4, 12, 6, 10, 7, 9, 5, 11, 2, 14, 3, 13, 1, 15)
    for o in order:
        c = spread(o)
        c.start()
        sent.append(c)
    load_own.wait()
    c = forward(0)
    c.start()
    sent.append(c)

    def store(block, values, lanes):
        halves = split(values)
        for first in (0, 1024):
            rows = pl.ds(pl.multiple_of(block * 64 + first, 64), 64)
            high[rows, lanes], low[rows, lanes] = halves

    mine, its = slice(0, 128), slice(128, 256)
    store(gx, own[gx], mine)
    for o in reversed(order):
        block = (gx + 16 - o) % 16
        spread(o).wait_recv()
        c = forward(o)
        c.start()
        sent.append(c)
        store(block, own[block], mine)
    for o in (0,) + order[::-1]:
        block = (gx + 16 - o) % 16
        remote(own.at[0], other.at[block], fw_send.at[o], fw_recv.at[o], mate).wait_recv()
        store(block, other[block], its)

    offs = []
    for q in range(4):
        o = [0]
        for s in range(4):
            bit = dims[(q + s) % 4][0]
            o.append(o[-1] + bit * (64 >> s))
        offs.append(o)

    def halve(q, s):
        half = 64 >> s
        bit, dev = dims[(q + s) % 4]
        row = pl.multiple_of(offs[q][s] + (1 - bit) * half, 8)
        return remote(part.at[q, pl.ds(row, half), :], rbufs[s].at[q],
                      rs_send.at[s, q], rs_recv.at[s, q], dev)

    top = core * 512
    for q in range(4):
        rows = pl.ds(pl.multiple_of(top + q * 128, 128), 128)
        window = pl.ds(pl.multiple_of(top + q * 128, 128), 640)
        part[q] = dot3((high[rows, :], low[rows, :]), (high[window, :], low[window, :]), ((1,), (1,)))
        c = halve(q, 0)
        c.start()
        sent.append(c)
    for s in range(4):
        half = 64 >> s
        for q in range(4):
            halve(q, s).wait_recv()
            keep = pl.ds(pl.multiple_of(offs[q][s + 1], 8), half)
            part[q, keep, :] = part[q, keep, :] + rbufs[s][q]
            if s < 3:
                c = halve(q, s + 1)
                c.start()
                sent.append(c)
    for n in range(24):
        q, lanes = n // 5, slice(128 * (n % 5), 128 * (n % 5) + 128)
        if n < 20:
            zout[n % 8, n // 8] = part[q, pl.ds(pl.multiple_of(offs[q][4], 8), 8), lanes]
        else:
            zout[n % 8, n // 8] = jnp.zeros((8, 128), jnp.float32)

    def zscatter(o):
        return remote(zout.at[(z + o) % 8], zin.at[o - 1], zr_send.at[o - 1], zr_recv.at[o - 1], zpeers[o - 1])
    def zgather(o):
        return remote(zall.at[0], zall.at[o], za_send.at[o - 1], za_recv.at[o - 1], zpeers[o - 1])
    for o in range(1, 8):
        c = zscatter(o)
        c.start()
        sent.append(c)
    total = zout[z]
    for o in range(1, 8):
        zscatter(o).wait_recv()
        total = total + zin[o - 1]
    zall[0] = total * scale
    for o in range(1, 8):
        c = zgather(o)
        c.start()
        sent.append(c)

    def at_row(q, row, size):
        return pl.ds(pl.multiple_of(top + q * 128 + row, 8), size)

    for o in range(1, 8):
        zgather(o).wait_recv()
    for n in range(20):
        q, lanes = n // 5, slice(128 * (n % 5), 128 * (n % 5) + 128)
        gsym[at_row(q, offs[q][4], 8), lanes] = zall[(z + 8 - n % 8) % 8, n // 8]

    def grow(q, s):
        ref = gsym.at[at_row(q, offs[q][s + 1], 64 >> s), :]
        return remote(ref, ref, ag_send.at[s, q], ag_recv.at[s, q], dims[(q + s) % 4][1])

    def hand(q, s):
        if s == 4:
            rows = at_row(q, offs[q][4], 8)
        else:
            half = 64 >> s
            rows = at_row(q, offs[q][s] + (1 - dims[(q + s) % 4][0]) * half, half)
        ref = gsym.at[rows, :]
        return remote(ref, ref, core_send.at[s, q], core_recv.at[s, q], mate)

    def take(q, s):
        if s == 4:
            row, size = offs[q][4], 8
        else:
            size = 64 >> s
            row = offs[q][s] + (1 - dims[(q + s) % 4][0]) * size
        ref = gsym.at[pl.ds(pl.multiple_of(512 - top + q * 128 + row, 8), size), :]
        return remote(ref, ref, core_send.at[s, q], core_recv.at[s, q], mate)

    for s in (3, 2, 1, 0):
        for q in range(4):
            if s < 3:
                grown = offs[q][s + 1] + (1 - dims[(q + s + 1) % 4][0]) * (64 >> (s + 1))
                ref = gsym.at[at_row(q, grown, 64 >> (s + 1)), :]
                remote(ref, ref, ag_send.at[s + 1, q], ag_recv.at[s + 1, q], mate).wait_recv()
            c = grow(q, s)
            c.start()
            sent.append(c)
            c = hand(q, s + 1)
            c.start()
            sent.append(c)
    def unpack(i):
        for b in range(5):
            j = (i + b) % 8
            block = gsym[pl.ds(pl.multiple_of(128 * i, 128), 128), 128 * b:128 * b + 128]
            spots = [(i, j, block)]
            if 0 < b < 4:
                spots.append((j, i, block.T))
            for row, col, value in spots:
                for n, piece in enumerate(thirds(value)):
                    gram[n, pl.ds(pl.multiple_of(128 * row, 128), 128),
                         pl.ds(pl.multiple_of(128 * col, 128), 128)] = piece

    for q in range(4):
        grown = offs[q][0] + (1 - dims[q % 4][0]) * 64
        ref = gsym.at[at_row(q, grown, 64), :]
        remote(ref, ref, ag_send.at[0, q], ag_recv.at[0, q], mate).wait_recv()
        c = hand(q, 0)
        c.start()
        sent.append(c)
        unpack(core * 4 + q)
    for q in range(4):
        for s in (4, 3, 2, 1, 0):
            take(q, s).wait_recv()
        unpack((1 - core) * 4 + q)

    rows, rank = q0_ref.shape
    tile = 256
    one = lambda u, v: jnp.dot(u, v, preferred_element_type=jnp.float32)

    def keep(at, values):
        for n, piece in enumerate(thirds(values)):
            parts_q[at, 128 * n:128 * n + 128] = piece

    load_start.wait()
    keep(slice(0, rows), q_ref[...])

    @pl.loop(0, iters)
    def _(it):
        @pl.loop(0, rows // tile)
        def _(t):
            at = pl.ds(pl.multiple_of(t * tile, tile), tile)
            big, mid, small = gram[0, at, :], gram[1, at, :], gram[2, at, :]
            both = parts_q[:, 0:256]
            wide = one(big, both) + one(mid, both)
            tiny = one(big, parts_q[:, 256:384]) + one(small, parts_q[:, 0:128])
            q_ref[at, :] = wide[:, 0:128] + (wide[:, 128:256] + tiny)

        keep(slice(0, rows), q_ref[...])

        @pl.loop(0, 2)
        def _(twice):
            inner = lambda u, v: lax.dot_general(u, v, (((0,), (0,)), ((), ())), preferred_element_type=jnp.float32)
            both = parts_q[:, 0:256]
            four = inner(both, both)
            cross = inner(parts_q[:, 0:128], parts_q[:, 256:384]) + four[0:128, 128:256]
            a_ref[...] = four[0:128, 0:128] + ((cross + cross.T) + four[128:256, 128:256])
            inverse_factor(a_ref, rank)
            f_big, f_mid, f_small = thirds(a_ref[...].T)
            main = jnp.concatenate([jnp.concatenate([f_big, f_big]), jnp.concatenate([f_mid, f_mid])], axis=1)
            wide = one(parts_q[:, 0:256], main)
            tiny = one(parts_q[:, 0:128], f_small) + one(parts_q[:, 256:384], f_big)
            q_ref[...] = wide[:, 0:128] + (wide[:, 128:256] + tiny)
            keep(slice(0, rows), q_ref[...])

    basis = (parts_q[:, 0:128], parts_q[:, 128:256])
    made = dot3(basis, (high[0:rows, :], low[0:rows, :]), ((0,), (0,)))
    share = rank // 4
    width = 128
    for t in range(4):
        proj[t, :, pl.ds(pl.multiple_of(core * width, width), width)] = made[t * share:(t + 1) * share, 0:width]
        proj[t, :, pl.ds(pl.multiple_of((1 - core) * width, width), width)] = made[t * share:(t + 1) * share, width:]
    zl = z % 2
    span = pl.ds(pl.multiple_of(zl * 2 * width, 2 * width), 2 * width)
    c = remote(proj.at[(1 - zl) * 2 + core], core_ref.at[:, span], last_sems.at[0], last_sems.at[1],
               device_at(x, y, z + 1 - 2 * zl, core))
    c.start()
    core_ref[:, span] = proj[gy]
    index = (gx * 4 + gy) * 4 + sa
    block = q_ref[pl.ds(pl.multiple_of((index // 2) * 8, 8), 8), :]
    flag = jnp.broadcast_to(index % 2, (4, rank))
    rows_ref[...] = jnp.where(flag == 0, block[0:4, :], block[4:8, :])
    c.wait_recv()
    sent.append(c)
    for c in sent:
        c.wait_send()


def whole(field, start, scale, iters):
    species, nx, width = field.shape[0], start.shape[0], field.shape[2]
    rank = start.shape[1]
    dma = lambda *shape: pltpu.SemaphoreType.DMA(shape)
    vm = lambda *shape: pltpu.VMEM(shape, jnp.float32)
    half = lambda *shape: pltpu.VMEM(shape, jnp.bfloat16)
    return pl.pallas_call(
        functools.partial(whole_body, scale, iters),
        out_shape=(jax.ShapeDtypeStruct((rank // 4, 4 * width), jnp.float32),
                   jax.ShapeDtypeStruct((nx // 256, rank), jnp.float32)),
        in_specs=[pl.BlockSpec(memory_space=pltpu.HBM)] * 2,
        out_specs=(pl.BlockSpec(memory_space=pltpu.VMEM),) * 2,
        scratch_shapes=[
            vm(16, 64, width), vm(16, 64, width), half(2 * nx, 2 * width), half(2 * nx, 2 * width),
            vm(4, 128, 640), vm(4, 64, 640), vm(4, 32, 640), vm(4, 16, 640), vm(4, 8, 640),
            vm(8, 3, 8, 128), vm(7, 3, 8, 128), vm(8, 3, 8, 128), vm(nx, 640),
            half(3, nx, nx), half(nx, 3 * rank), vm(nx, rank), vm(rank, rank), vm(4, rank // 4, 2 * width),
            dma(15), dma(15), dma(16), dma(16), dma(4, 4), dma(4, 4), dma(7), dma(7), dma(7), dma(7),
            dma(4, 4), dma(4, 4), dma(5, 4), dma(5, 4), dma(2), dma(2),
        ],
        compiler_params=pltpu.CompilerParams(collective_id=0, has_side_effects=True,
                                             vmem_limit_bytes=48 * 1024 * 1024),
        name="whole",
    )(field, start)


def on_device(scalar_field, start_basis):
    species, steps, rows, width = scalar_field.shape
    total_cols = width * lax.axis_size("gy") * S * steps
    core_tensor, own_rows = whole(scalar_field.reshape(species, rows, width), start_basis, 1.0 / total_cols, ITERS)
    return (core_tensor.reshape(1, steps, *core_tensor.shape), own_rows)


def solution(mesh):
    placed = (P("sa", None, "gx", "gy"), P())
    return jax.shard_map(
        on_device,
        mesh=mesh,
        in_specs=placed,
        out_specs=(P(("sa", "gx"), None, "gy", None), P(("gx", "gy", "sa"), None)),
        check_vma=False,
    )
```

```python
import functools

import jax
import jax.numpy as jnp
from jax import lax
from jax.experimental import pallas as pl
from jax.experimental.pallas import tpu as pltpu
from jax.sharding import PartitionSpec as P

NX = 1024
S = 64
ITERS = 3

TOP = float(jnp.finfo(jnp.float32).max)
MESH = pl.DeviceIdType.MESH

def place():
    gx, gy, sa = lax.axis_index("gx"), lax.axis_index("gy"), lax.axis_index("sa")
    return gx // 4, sa, (gx % 4) * 2 + gy // 2, gy % 2

def device_at(x, y, z, core):
    return {"gx": x * 4 + z // 2, "gy": (z % 2) * 2 + core, "sa": y}


def row_of(v, p):
    return jnp.broadcast_to(v[p:p + 1, :], v.shape)

def lane_of(v, c):
    return jnp.minimum(jnp.broadcast_to(v[:, c:c + 1], v.shape), TOP)

def inverse_factor(a_ref, rank):
    sub = lax.broadcasted_iota(jnp.int32, (8, rank), 0)
    lane = lax.broadcasted_iota(jnp.int32, (8, rank), 1)
    panels = rank // 8
    for k in range(panels):
        base = 8 * k
        more = k + 1 < panels
        panel = a_ref[base:base + 8, :]
        cols = [lane_of(panel, base + c) for c in range(8)]
        inside = (lane >= base) & (lane < base + 8)
        panel = jnp.where(inside, jnp.where(lane - base == sub, 1.0, 0.0), panel)
        if more:
            nxt = a_ref[base + 8:base + 16, :]
            ncols = [lane_of(nxt, base + c) for c in range(8)]
            nxt = jnp.where(inside, 0.0, nxt)
        diag = jnp.zeros((8, rank), jnp.float32)
        for p in range(8):
            d = row_of(cols[p], p)
            r = 1.0 / d
            diag = jnp.where(sub == p, d, diag)
            f = jnp.where(sub > p, cols[p] * r, 0.0)
            prow = row_of(panel, p)
            if more:
                g = ncols[p] * r
                nxt = nxt - g * prow
            if p < 7:
                for c in range(p + 1, 8):
                    crow = row_of(cols[c], p)
                    cols[c] = cols[c] - f * crow
                    if more:
                        ncols[c] = ncols[c] - g * crow
                panel = panel - f * prow
        root = lax.rsqrt(diag)
        scaled = panel * root
        a_ref[base:base + 8, :] = jnp.where(lane < base + 8, scaled, 0.0)
        if more:
            a_ref[base + 8:base + 16, :] = nxt
        if k + 2 < panels:
            low = base + 16
            upper = jnp.where(lane >= low, scaled, 0.0)
            left, right = thirds(upper), thirds(scaled)
            pick = lambda v, order: jnp.concatenate([v[n].astype(jnp.float32) for n in order]).astype(jnp.bfloat16)
            upd = lax.dot_general(pick(left, (0, 0, 1, 1, 0, 2)), pick(right, (0, 1, 0, 1, 2, 0)),
                                  (((0,), (0,)), ((), ())), preferred_element_type=jnp.float32)
            rest = a_ref[low:, :]
            lanes = lax.broadcasted_iota(jnp.int32, rest.shape, 1)
            rest = jnp.where((lanes >= base) & (lanes < base + 8), 0.0, rest)
            a_ref[low:, :] = rest - upd[low:, :]


def split(v):
    high = v.astype(jnp.bfloat16)
    return high, (v - high.astype(jnp.float32)).astype(jnp.bfloat16)


def thirds(v):
    big, rest = v.astype(jnp.bfloat16), v
    rest = rest - big.astype(jnp.float32)
    mid = rest.astype(jnp.bfloat16)
    return big, mid, (rest - mid.astype(jnp.float32)).astype(jnp.bfloat16)


def dot3(a, b, contract):
    one = lambda u, v: lax.dot_general(u, v, (contract, ((), ())), preferred_element_type=jnp.float32)
    return one(a[0], b[0]) + (one(a[0], b[1]) + one(a[1], b[0]))


def whole_body(scale, iters, field_ref, q0_ref, core_ref, rows_ref, own, other, high, low, part, r0, r1, r2, r3,
               zout, zin, zall, gsym, gram, parts_q, q_ref, a_ref, proj,
               fs_send, fs_recv, fw_send, fw_recv, rs_send, rs_recv, zr_send, zr_recv, za_send, za_recv,
               ag_send, ag_recv, core_send, core_recv, last_sems, local_sems):
    x, y, z, core = place()
    rbufs = (r0, r1, r2, r3)
    mate = device_at(x, y, z, 1 - core)
    pair = lambda i: i + 1 - 2 * (i % 2)
    dims = (
        (((x + 1) // 2) % 2, device_at(pair(x), y, z, core)),
        (((y + 1) // 2) % 2, device_at(x, pair(y), z, core)),
        (x // 2, device_at(3 - x, y, z, core)),
        (y // 2, device_at(x, 3 - y, z, core)),
    )
    zpeers = [device_at(x, y, (z + o) % 8, core) for o in range(1, 8)]

    load_own = pltpu.make_async_copy(field_ref.at[lax.axis_index("gx")], own.at[lax.axis_index("gx")],
                                     local_sems.at[0])
    load_own.start()
    load_start = pltpu.make_async_copy(q0_ref, q_ref, local_sems.at[1])
    load_start.start()
    barrier = pltpu.get_barrier_semaphore()
    gx, gy, sa = lax.axis_index("gx"), lax.axis_index("gy"), lax.axis_index("sa")
    xpeers = [{"gx": (gx + o) % 16, "gy": gy, "sa": sa} for o in range(1, 16)]
    peers = [mate, dims[1][1], dims[3][1]] + zpeers[0::2] + xpeers
    for peer in peers:
        pl.semaphore_signal(barrier, inc=1, device_id=peer, device_id_type=MESH)
    pl.semaphore_wait(barrier, len(peers))

    def remote(src, dst, ss, rs, dev):
        return pltpu.make_async_remote_copy(src_ref=src, dst_ref=dst, send_sem=ss, recv_sem=rs,
                                            device_id=dev, device_id_type=MESH)
    sent = []

    def spread(o):
        return remote(field_ref.at[(gx + o) % 16], own.at[gx], fs_send.at[o - 1], fs_recv.at[o - 1], xpeers[o - 1])

    def forward(o):
        block = (gx + 16 - o) % 16
        return remote(own.at[block], other.at[block], fw_send.at[o], fw_recv.at[o], mate)

    order = (8, 4, 12, 6, 10, 7, 9, 5, 11, 2, 14, 3, 13, 1, 15)
    for o in order:
        c = spread(o)
        c.start()
        sent.append(c)
    load_own.wait()
    c = forward(0)
    c.start()
    sent.append(c)

    def store(block, values, lanes):
        halves = split(values)
        for first in (0, 1024):
            rows = pl.ds(pl.multiple_of(block * 64 + first, 64), 64)
            high[rows, lanes], low[rows, lanes] = halves

    mine, its = slice(0, 128), slice(128, 256)
    store(gx, own[gx], mine)
    for o in reversed(order):
        block = (gx + 16 - o) % 16
        spread(o).wait_recv()
        c = forward(o)
        c.start()
        sent.append(c)
        store(block, own[block], mine)
    for o in (0,) + order[::-1]:
        block = (gx + 16 - o) % 16
        remote(own.at[0], other.at[block], fw_send.at[o], fw_recv.at[o], mate).wait_recv()
        store(block, other[block], its)

    offs = []
    for q in range(4):
        o = [0]
        for s in range(4):
            bit = dims[(q + s) % 4][0]
            o.append(o[-1] + bit * (64 >> s))
        offs.append(o)

    def halve(q, s):
        half = 64 >> s
        bit, dev = dims[(q + s) % 4]
        row = pl.multiple_of(offs[q][s] + (1 - bit) * half, 8)
        return remote(part.at[q, pl.ds(row, half), :], rbufs[s].at[q],
                      rs_send.at[s, q], rs_recv.at[s, q], dev)

    top = core * 512
    for q in range(4):
        rows = pl.ds(pl.multiple_of(top + q * 128, 128), 128)
        window = pl.ds(pl.multiple_of(top + q * 128, 128), 640)
        part[q] = dot3((high[rows, :], low[rows, :]), (high[window, :], low[window, :]), ((1,), (1,)))
        c = halve(q, 0)
        c.start()
        sent.append(c)
    for s in range(4):
        half = 64 >> s
        for q in range(4):
            halve(q, s).wait_recv()
            keep = pl.ds(pl.multiple_of(offs[q][s + 1], 8), half)
            part[q, keep, :] = part[q, keep, :] + rbufs[s][q]
            if s < 3:
                c = halve(q, s + 1)
                c.start()
                sent.append(c)
    for n in range(24):
        q, lanes = n // 5, slice(128 * (n % 5), 128 * (n % 5) + 128)
        if n < 20:
            zout[n % 8, n // 8] = part[q, pl.ds(pl.multiple_of(offs[q][4], 8), 8), lanes]
        else:
            zout[n % 8, n // 8] = jnp.zeros((8, 128), jnp.float32)

    def zscatter(o):
        return remote(zout.at[(z + o) % 8], zin.at[o - 1], zr_send.at[o - 1], zr_recv.at[o - 1], zpeers[o - 1])
    def zgather(o):
        return remote(zall.at[0], zall.at[o], za_send.at[o - 1], za_recv.at[o - 1], zpeers[o - 1])
    for o in range(1, 8):
        c = zscatter(o)
        c.start()
        sent.append(c)
    total = zout[z]
    for o in range(1, 8):
        zscatter(o).wait_recv()
        total = total + zin[o - 1]
    zall[0] = total * scale
    for o in range(1, 8):
        c = zgather(o)
        c.start()
        sent.append(c)

    def at_row(q, row, size):
        return pl.ds(pl.multiple_of(top + q * 128 + row, 8), size)

    for o in range(1, 8):
        zgather(o).wait_recv()
    for n in range(20):
        q, lanes = n // 5, slice(128 * (n % 5), 128 * (n % 5) + 128)
        gsym[at_row(q, offs[q][4], 8), lanes] = zall[(z + 8 - n % 8) % 8, n // 8]

    def grow(q, s):
        ref = gsym.at[at_row(q, offs[q][s + 1], 64 >> s), :]
        return remote(ref, ref, ag_send.at[s, q], ag_recv.at[s, q], dims[(q + s) % 4][1])

    def hand(q, s):
        if s == 4:
            rows = at_row(q, offs[q][4], 8)
        else:
            half = 64 >> s
            rows = at_row(q, offs[q][s] + (1 - dims[(q + s) % 4][0]) * half, half)
        ref = gsym.at[rows, :]
        return remote(ref, ref, core_send.at[s, q], core_recv.at[s, q], mate)

    def take(q, s):
        if s == 4:
            row, size = offs[q][4], 8
        else:
            size = 64 >> s
            row = offs[q][s] + (1 - dims[(q + s) % 4][0]) * size
        ref = gsym.at[pl.ds(pl.multiple_of(512 - top + q * 128 + row, 8), size), :]
        return remote(ref, ref, core_send.at[s, q], core_recv.at[s, q], mate)

    for s in (3, 2, 1, 0):
        for q in range(4):
            if s < 3:
                grown = offs[q][s + 1] + (1 - dims[(q + s + 1) % 4][0]) * (64 >> (s + 1))
                ref = gsym.at[at_row(q, grown, 64 >> (s + 1)), :]
                remote(ref, ref, ag_send.at[s + 1, q], ag_recv.at[s + 1, q], mate).wait_recv()
            c = grow(q, s)
            c.start()
            sent.append(c)
            c = hand(q, s + 1)
            c.start()
            sent.append(c)
    def unpack(i):
        for b in range(5):
            j = (i + b) % 8
            block = gsym[pl.ds(pl.multiple_of(128 * i, 128), 128), 128 * b:128 * b + 128]
            spots = [(i, j, block)]
            if 0 < b < 4:
                spots.append((j, i, block.T))
            for row, col, value in spots:
                for n, piece in enumerate(thirds(value)):
                    gram[n, pl.ds(pl.multiple_of(128 * row, 128), 128),
                         pl.ds(pl.multiple_of(128 * col, 128), 128)] = piece

    for q in range(4):
        grown = offs[q][0] + (1 - dims[q % 4][0]) * 64
        ref = gsym.at[at_row(q, grown, 64), :]
        remote(ref, ref, ag_send.at[0, q], ag_recv.at[0, q], mate).wait_recv()
        c = hand(q, 0)
        c.start()
        sent.append(c)
        unpack(core * 4 + q)
    for q in range(4):
        for s in (4, 3, 2, 1, 0):
            take(q, s).wait_recv()
        unpack((1 - core) * 4 + q)

    rows, rank = q0_ref.shape
    tile = 512
    one = lambda u, v: jnp.dot(u, v, preferred_element_type=jnp.float32)

    def keep(at, values):
        for n, piece in enumerate(thirds(values)):
            parts_q[at, 128 * n:128 * n + 128] = piece

    load_start.wait()
    keep(slice(0, rows), q_ref[...])

    @pl.loop(0, iters)
    def _(it):
        @pl.loop(0, rows // tile)
        def _(t):
            at = pl.ds(pl.multiple_of(t * tile, tile), tile)
            big, mid, small = gram[0, at, :], gram[1, at, :], gram[2, at, :]
            both = parts_q[:, 0:256]
            wide = one(big, both) + one(mid, both)
            tiny = one(big, parts_q[:, 256:384]) + one(small, parts_q[:, 0:128])
            q_ref[at, :] = wide[:, 0:128] + (wide[:, 128:256] + tiny)

        keep(slice(0, rows), q_ref[...])

        @pl.loop(0, 2)
        def _(twice):
            inner = lambda u, v: lax.dot_general(u, v, (((0,), (0,)), ((), ())), preferred_element_type=jnp.float32)
            both = parts_q[:, 0:256]
            four = inner(both, both)
            cross = inner(parts_q[:, 0:128], parts_q[:, 256:384]) + four[0:128, 128:256]
            a_ref[...] = four[0:128, 0:128] + ((cross + cross.T) + four[128:256, 128:256])
            inverse_factor(a_ref, rank)
            f_big, f_mid, f_small = thirds(a_ref[...].T)
            main = jnp.concatenate([jnp.concatenate([f_big, f_big]), jnp.concatenate([f_mid, f_mid])], axis=1)
            wide = one(parts_q[:, 0:256], main)
            tiny = one(parts_q[:, 0:128], f_small) + one(parts_q[:, 256:384], f_big)
            q_ref[...] = wide[:, 0:128] + (wide[:, 128:256] + tiny)
            keep(slice(0, rows), q_ref[...])

    basis = (parts_q[:, 0:128], parts_q[:, 128:256])
    made = dot3(basis, (high[0:rows, :], low[0:rows, :]), ((0,), (0,)))
    share = rank // 4
    width = 128
    for t in range(4):
        proj[t, :, pl.ds(pl.multiple_of(core * width, width), width)] = made[t * share:(t + 1) * share, 0:width]
        proj[t, :, pl.ds(pl.multiple_of((1 - core) * width, width), width)] = made[t * share:(t + 1) * share, width:]
    zl = z % 2
    span = pl.ds(pl.multiple_of(zl * 2 * width, 2 * width), 2 * width)
    c = remote(proj.at[(1 - zl) * 2 + core], core_ref.at[:, span], last_sems.at[0], last_sems.at[1],
               device_at(x, y, z + 1 - 2 * zl, core))
    c.start()
    core_ref[:, span] = proj[gy]
    index = (gx * 4 + gy) * 4 + sa
    block = q_ref[pl.ds(pl.multiple_of((index // 2) * 8, 8), 8), :]
    flag = jnp.broadcast_to(index % 2, (4, rank))
    rows_ref[...] = jnp.where(flag == 0, block[0:4, :], block[4:8, :])
    c.wait_recv()
    sent.append(c)
    for c in sent:
        c.wait_send()


def whole(field, start, scale, iters):
    species, nx, width = field.shape[0], start.shape[0], field.shape[2]
    rank = start.shape[1]
    dma = lambda *shape: pltpu.SemaphoreType.DMA(shape)
    vm = lambda *shape: pltpu.VMEM(shape, jnp.float32)
    half = lambda *shape: pltpu.VMEM(shape, jnp.bfloat16)
    return pl.pallas_call(
        functools.partial(whole_body, scale, iters),
        out_shape=(jax.ShapeDtypeStruct((rank // 4, 4 * width), jnp.float32),
                   jax.ShapeDtypeStruct((nx // 256, rank), jnp.float32)),
        in_specs=[pl.BlockSpec(memory_space=pltpu.HBM)] * 2,
        out_specs=(pl.BlockSpec(memory_space=pltpu.VMEM),) * 2,
        scratch_shapes=[
            vm(16, 64, width), vm(16, 64, width), half(2 * nx, 2 * width), half(2 * nx, 2 * width),
            vm(4, 128, 640), vm(4, 64, 640), vm(4, 32, 640), vm(4, 16, 640), vm(4, 8, 640),
            vm(8, 3, 8, 128), vm(7, 3, 8, 128), vm(8, 3, 8, 128), vm(nx, 640),
            half(3, nx, nx), half(nx, 3 * rank), vm(nx, rank), vm(rank, rank), vm(4, rank // 4, 2 * width),
            dma(15), dma(15), dma(16), dma(16), dma(4, 4), dma(4, 4), dma(7), dma(7), dma(7), dma(7),
            dma(4, 4), dma(4, 4), dma(5, 4), dma(5, 4), dma(2), dma(2),
        ],
        compiler_params=pltpu.CompilerParams(collective_id=0, has_side_effects=True,
                                             vmem_limit_bytes=48 * 1024 * 1024),
        name="whole",
    )(field, start)


def on_device(scalar_field, start_basis):
    species, steps, rows, width = scalar_field.shape
    total_cols = width * lax.axis_size("gy") * S * steps
    core_tensor, own_rows = whole(scalar_field.reshape(species, rows, width), start_basis, 1.0 / total_cols, ITERS)
    return (core_tensor.reshape(1, steps, *core_tensor.shape), own_rows)


def solution(mesh):
    placed = (P("sa", None, "gx", "gy"), P())
    return jax.shard_map(
        on_device,
        mesh=mesh,
        in_specs=placed,
        out_specs=(P(("sa", "gx"), None, "gy", None), P(("gx", "gy", "sa"), None)),
        check_vma=False,
    )
```
